512 devices in a mesh: row: 16 (over x_lo, z), col: 32 (over x_hi, y, core).
Axes of the slice: x: 4 (x_hi: 2, x_lo: 2; x = x_hi * 2 + x_lo), y: 8, z: 8, core: 2. Of those that a mesh axis runs over, the one named last changes fastest.
Arguments:
- queries: bfloat16 [16, 1024, 512], P('row', 'col'), may hold values from -6 to 6
- keys: bfloat16 [32, 512, 512], P('col', 'row'), may hold values from -6 to 6
- values: bfloat16 [32, 512, 512], P('col', 'row'), may hold values from -6 to 6
- outputs: bfloat16 [16, 1024, 512], P('row', 'col'), may hold values from -2 to 2
- grad_out: bfloat16 [16, 1024, 512], P('row', 'col'), may hold values from -48 to 48
- lse: float32 [16, 8, 1024], P('row'), may hold values from 7 to 9.5
- tile_slot: int32 [16, 32, 24], P('row', 'col'), may hold values from 0 to 31, as said below
- tile_live: int32 [16, 32], P('row', 'col'), may hold values from 1 to 24, as said below
- tile_bits: int32 [16, 32, 24, 8, 128], P('row', 'col'), may hold values from 0 to 65535, as said below
Outputs:
- grad_queries: bfloat16 [16, 1024, 512], P('row', 'col')
- grad_keys: bfloat16 [32, 512, 512], P('col', 'row')
- grad_values: bfloat16 [32, 512, 512], P('col', 'row')
The draws below stay inside these ranges and needn't reach their ends.
Inputs may be any that keep to these rules, and one draw needn't show every extreme that they name: `tile_slot`: the 24 entries of one pair of blocks are distinct slots. `tile_live`: some pair of blocks has all 24 entries live. `tile_bits`: each word holds 16 edge bits in its low bits.
All inputs are finite; a program needn't handle non-finite values.
Results may differ from the reference program's by a relative error of at most 0.02.
Values may be sent and summed in bfloat16 or wider, within the bound.
A program may use at most 64 MiB of HBM per device.

```python
import jax
import jax.numpy as jnp
from jax import lax

HEADS = 8
D = 512
TILE = 128
QROWS = 1024
QBLOCKS = 16
KBLOCKS = 32
KCOLS = 512
CAP = 24


def draw_tile_slot(key, part):
    slot_total = QROWS // TILE * (KCOLS // TILE)
    block_keys = jax.random.split(key, QBLOCKS * KBLOCKS)
    orders = jax.vmap(lambda one_key: jax.random.permutation(one_key, slot_total))(block_keys)
    return orders[:, :CAP].reshape(QBLOCKS, KBLOCKS, CAP).astype(jnp.int32)


def draw_tile_live(key, part):
    key_one, key_two = jax.random.split(key)
    spread = jax.random.randint(key_one, (QBLOCKS, KBLOCKS), 0, CAP, dtype=jnp.int32)
    counts = 1 + spread * spread // CAP
    chosen = jax.random.randint(key_two, (), 0, QBLOCKS * KBLOCKS, dtype=jnp.int32)
    positions = jnp.arange(QBLOCKS * KBLOCKS, dtype=jnp.int32).reshape(QBLOCKS, KBLOCKS)
    return jnp.where(positions == chosen, CAP, counts).astype(jnp.int32)


def draw_tile_bits(key, part):
    words = jax.random.randint(key, (QBLOCKS, KBLOCKS, CAP, TILE // 16, TILE), 0, 65536, dtype=jnp.int32)
    words = words.at[0, 0, 0, 0, 0].set(jnp.int32(65535))
    words = words.at[0, 0, 0, 0, 1].set(jnp.int32(0))
    return words.astype(jnp.int32)


def level_of(own_key, dims, cuts, smallest, largest):
    def one(dim, parts):
        heights = jax.random.uniform(jax.random.fold_in(jax.random.fold_in(own_key, 6), dim), (parts,), jnp.float32, smallest / len(cuts), largest / len(cuts))
        return jnp.repeat(jnp.exp(heights), dims[dim] // parts).reshape((-1,) + (1,) * (len(dims) - dim - 1))

    level = one(*cuts[0])
    for cut in cuts[1:]:
        level = level * one(*cut)
    return level


def bell_draw(key, dims, width, bound, pieces=(), held_as=jnp.bfloat16):
    factor_of = level_of(key, dims, pieces, -0.22, 0.18) if pieces else 1.0
    result = jax.random.normal(key, dims, jnp.float32) * width * factor_of
    return jnp.minimum(jnp.maximum(result, -bound), bound).astype(held_as)


def setup_inputs(seed: int = 0) -> dict:
    splits = jax.random.split(jax.random.key(seed), 10)
    queries = bell_draw(splits[0], (QBLOCKS, QROWS, D), 1.0, 6.0, ((0, 16), (1, 32)))
    keys = bell_draw(splits[1], (KBLOCKS, KCOLS, D), 1.0, 6.0, ((0, 32), (1, 16)))
    values = bell_draw(splits[2], (KBLOCKS, KCOLS, D), 1.0, 6.0, ((0, 32), (1, 16)))
    outputs = bell_draw(splits[3], (QBLOCKS, QROWS, D), 0.3, 2.0, ((0, 16), (1, 32)))
    grad_out = bell_draw(splits[4], (QBLOCKS, QROWS, D), 8.0, 48.0, ((0, 16), (1, 32)))
    lse = jnp.clip(7.0 + 2.5 * jax.random.uniform(splits[5], (QBLOCKS, HEADS, QROWS), jnp.float32) ** level_of(splits[5], (QBLOCKS, HEADS, QROWS), ((0, 16),), -0.2, 0.2), 7.0, 9.5)
    tile_slot = draw_tile_slot(jax.random.fold_in(splits[9], 71), 0)
    tile_live = draw_tile_live(jax.random.fold_in(splits[9], 71), 0)
    tile_bits = draw_tile_bits(jax.random.fold_in(splits[9], 71), 0)
    return {"queries": queries, "keys": keys, "values": values, "outputs": outputs, "grad_out": grad_out, "lse": lse, "tile_slot": tile_slot, "tile_live": tile_live, "tile_bits": tile_bits}


def unpack_bits(packed_rows):
    shifts = jnp.arange(16, dtype=jnp.int32)
    bit_values = jnp.bitwise_and(jnp.right_shift(packed_rows[:, :, None], shifts), 1)
    return jnp.transpose(bit_values, (1, 0, 2)).reshape(packed_rows.shape[1], packed_rows.shape[0] * 16) == 1


def row_delta(grads, outs, head_count):
    leading = grads.shape[:-1]
    model_width = grads.shape[-1]
    product = (grads.astype(jnp.float32) * outs.astype(jnp.float32)).reshape(leading + (head_count, model_width // head_count))
    return jnp.swapaxes(jnp.sum(product, axis=-1), -1, -2).astype(jnp.bfloat16)


def add_rows(total, piece, start):
    current = lax.dynamic_slice_in_dim(total, start, piece.shape[0], 0)
    return lax.dynamic_update_slice_in_dim(total, current + piece, start, 0)


def add_block(total, piece, block_col, start):
    zero_index = jnp.int32(0)
    current = lax.dynamic_slice(total, (block_col, start, zero_index), (1, piece.shape[0], piece.shape[1]))
    return lax.dynamic_update_slice(total, current + piece[None], (block_col, start, zero_index))


def reference(queries, keys, values, outputs, grad_out, lse, tile_slot, tile_live, tile_bits):
    block_rows = queries.shape[0]
    query_count = queries.shape[1]
    model_width = queries.shape[2]
    block_cols = keys.shape[0]
    key_count = keys.shape[1]
    head_count = lse.shape[1]
    head_dim = model_width // head_count
    tile_size = tile_bits.shape[4]
    capacity = tile_slot.shape[2]
    key_tiles = key_count // tile_size
    scaling = float(head_dim) ** -0.5
    highest = lax.Precision.HIGHEST
    delta_all = lax.optimization_barrier(row_delta(grad_out, outputs, head_count)).astype(jnp.float32)

    def per_block(block_row, state):
        grad_q_all, grad_k_all, grad_v_all = state
        block_row = block_row.astype(jnp.int32)
        query_block = lax.dynamic_index_in_dim(queries, block_row, 0, keepdims=False).astype(jnp.float32)
        grad_block = lax.dynamic_index_in_dim(grad_out, block_row, 0, keepdims=False).astype(jnp.float32)
        lse_block = lax.dynamic_index_in_dim(lse, block_row, 0, keepdims=False)
        delta_block = lax.dynamic_index_in_dim(delta_all, block_row, 0, keepdims=False)

        def per_tile(flat_index, running):
            flat_index = flat_index.astype(jnp.int32)
            block_col = flat_index // capacity
            entry_index = flat_index % capacity
            slot_value = tile_slot[block_row, block_col, entry_index]
            live_count = tile_live[block_row, block_col]

            def compute(partial_sums):
                grad_q, grad_k, grad_v = partial_sums
                q_start = (slot_value // key_tiles) * tile_size
                k_start = (slot_value % key_tiles) * tile_size
                zero_index = jnp.int32(0)
                q_tile = lax.dynamic_slice_in_dim(query_block, q_start, tile_size, 0).reshape(tile_size, head_count, head_dim)
                g_tile = lax.dynamic_slice_in_dim(grad_block, q_start, tile_size, 0).reshape(tile_size, head_count, head_dim)
                k_tile = lax.dynamic_slice(keys, (block_col, k_start, zero_index), (1, tile_size, model_width))[0]
                k_tile = k_tile.astype(jnp.float32).reshape(tile_size, head_count, head_dim)
                v_tile = lax.dynamic_slice(values, (block_col, k_start, zero_index), (1, tile_size, model_width))[0]
                v_tile = v_tile.astype(jnp.float32).reshape(tile_size, head_count, head_dim)
                lse_tile = lax.dynamic_slice_in_dim(lse_block, q_start, tile_size, 1)
                delta_tile = lax.dynamic_slice_in_dim(delta_block, q_start, tile_size, 1)
                edge_mask = unpack_bits(tile_bits[block_row, block_col, entry_index])
                scores = jnp.einsum("ihd,jhd->hij", q_tile, k_tile, precision=highest) * scaling
                attn_prob = jnp.where(edge_mask[None], jnp.exp(scores - lse_tile[:, :, None]), 0.0)
                prob_low = lax.optimization_barrier(attn_prob.astype(jnp.bfloat16)).astype(jnp.float32)
                value_tile_grad = jnp.einsum("hij,ihd->jhd", prob_low, g_tile, precision=highest).reshape(tile_size, model_width)
                grad_prob = jnp.einsum("ihd,jhd->hij", g_tile, v_tile, precision=highest)
                score_grad = attn_prob * (grad_prob - delta_tile[:, :, None])
                score_low = lax.optimization_barrier(score_grad.astype(jnp.bfloat16)).astype(jnp.float32)
                query_tile_grad = jnp.einsum("hij,jhd->ihd", score_low, k_tile, precision=highest).reshape(tile_size, model_width) * scaling
                key_tile_grad = jnp.einsum("hij,ihd->jhd", score_low, q_tile, precision=highest).reshape(tile_size, model_width) * scaling
                grad_q = add_rows(grad_q, query_tile_grad, q_start)
                grad_k = add_block(grad_k, key_tile_grad, block_col, k_start)
                grad_v = add_block(grad_v, value_tile_grad, block_col, k_start)
                return (grad_q, grad_k, grad_v)

            return lax.cond(entry_index < live_count, compute, lambda unchanged: unchanged, running)

        start_sums = (jnp.zeros((query_count, model_width), jnp.float32), jnp.zeros(keys.shape, jnp.float32), jnp.zeros(keys.shape, jnp.float32))
        grad_q, grad_k, grad_v = lax.fori_loop(0, block_cols * capacity, per_tile, start_sums)
        grad_q_all = lax.dynamic_update_index_in_dim(grad_q_all, grad_q, block_row, 0)
        grad_k_all = grad_k_all + lax.optimization_barrier(grad_k.astype(jnp.bfloat16)).astype(jnp.float32)
        grad_v_all = grad_v_all + lax.optimization_barrier(grad_v.astype(jnp.bfloat16)).astype(jnp.float32)
        return (grad_q_all, grad_k_all, grad_v_all)

    initial = (jnp.zeros(queries.shape, jnp.float32), jnp.zeros(keys.shape, jnp.float32), jnp.zeros(keys.shape, jnp.float32))
    grad_q_all, grad_k_all, grad_v_all = lax.fori_loop(0, block_rows, per_block, initial)
    return (grad_q_all.astype(jnp.bfloat16), grad_k_all.astype(jnp.bfloat16), grad_v_all.astype(jnp.bfloat16))
```

```python
import functools
import math

import jax
import jax.numpy as jnp
from jax import lax
from jax.experimental import pallas as pl
from jax.experimental.pallas import tpu as pltpu
from jax.sharding import PartitionSpec as P

MESH = pl.DeviceIdType.MESH
RING = 8
PIECE = 32
NEG = -1e30
F32 = jnp.float32
BF16 = jnp.bfloat16


def places():
    r, col = lax.axis_index("row"), lax.axis_index("col")
    xl, z = r // RING, lax.rem(r, RING)
    c = lax.rem(col, 2)
    y = lax.rem(col // 2, RING)
    xh = col // (2 * RING)
    return xl, z, xh, y, c


def turn(a, d):
    return lax.rem(a + d + RING, RING)


def q_rows(xh, y, c):
    return pl.ds(pl.multiple_of((xh * 16 + y * 2 + c) * PIECE, PIECE), PIECE)


def k_rows(xl, z):
    return pl.ds(pl.multiple_of((xl * 8 + z) * PIECE, PIECE), PIECE)


def neighbours(xl, z, xh, y, c):
    def on_col(xh, y, c):
        return {"col": xh * 16 + y * 2 + c}

    def on_row(xl, z):
        return {"row": xl * 8 + z}

    return {
        "qx": on_col(1 - xh, y, c),
        "qc": on_col(xh, y, 1 - c),
        "q+": on_col(xh, turn(y, 1), c),
        "q-": on_col(xh, turn(y, -1), c),
        "kx": on_row(1 - xl, z),
        "k+": on_row(xl, turn(z, 1)),
        "k-": on_row(xl, turn(z, -1)),
    }


def greet(near):
    barrier = pltpu.get_barrier_semaphore()
    for where in near.values():
        pl.semaphore_signal(barrier, inc=1, device_id=where, device_id_type=MESH)
    pl.semaphore_wait(barrier, len(near))


class Post:
    def __init__(self, send, recv):
        self.send, self.recv, self.count, self.sent = send, recv, 0, []

    def slot(self):
        self.count += 1
        return self.count - 1

    def put(self, slot, src, dst, where):
        copy = pltpu.make_async_remote_copy(
            src_ref=src,
            dst_ref=dst,
            send_sem=self.send.at[slot],
            recv_sem=self.recv.at[slot],
            device_id=where,
            device_id_type=MESH,
        )
        copy.start()
        self.sent.append(copy)

    def got(self, slot, dst):
        pltpu.make_async_copy(dst, dst, self.recv.at[slot]).wait()

    def finish(self):
        for copy in self.sent:
            copy.wait_send()


def gather_kernel(q, g, o, k, v, qa, ga, ka, va, own_g, own_sem, send, recv):
    xl, z, xh, y, c = places()
    near = neighbours(xl, z, xh, y, c)
    greet(near)
    post = Post(send, recv)

    def spread(kind, own, full, rows_of, here, reach):
        pos, ring = here
        slots = {}
        for s in ("own", "mate"):
            for sign, far in reach:
                for d in range(1, far + 1):
                    slots[s, sign, d] = post.slot()
        slots["mate"] = post.slot()
        return dict(kind=kind, own=own, full=full, rows=rows_of, pos=pos, ring=ring, reach=reach, slots=slots)

    long_plus = ((1, 4), (-1, 3))
    long_minus = ((1, 3), (-1, 4))
    q_of = lambda x, t, core: q_rows(x, t, core)
    k_of = lambda x, t, core: k_rows(x, t)
    streams = [
        spread("k", k, ka, k_of, (xl, z), long_plus),
        spread("q", q, qa, q_of, (xh, y), long_plus),
        spread("k", v, va, k_of, (xl, z), long_minus),
        spread("q", own_g, ga, q_of, (xh, y), long_minus),
    ]
    for st in streams:
        if st["kind"] == "q":
            st["core"] = {}
            for s in ("own", "mate"):
                st["core"][s, 0] = post.slot()
                for sign, far in st["reach"]:
                    for d in range(1, far + 1):
                        st["core"][s, sign * d] = post.slot()

    def part_of(st, s):
        return st["pos"] if s == "own" else 1 - st["pos"]

    def ring_send(st, s, sign, d, src):
        rows = st["rows"](part_of(st, s), turn(st["ring"], -sign * (d - 1)), c)
        if src is None:
            src = st["full"].at[rows]
        way = st["kind"] + ("+" if sign > 0 else "-")
        post.put(st["slots"][s, sign, d], src, st["full"].at[rows], near[way])

    def core_send(st, s, shift, src):
        if st["kind"] != "q":
            return
        rows = st["rows"](part_of(st, s), turn(st["ring"], -shift), c)
        if src is None:
            src = st["full"].at[rows]
        post.put(st["core"][s, shift], src, st["full"].at[rows], near["qc"])

    def begin(st):
        rows = st["rows"](st["pos"], st["ring"], c)
        post.put(st["slots"]["mate"], st["own"], st["full"].at[rows], near[st["kind"] + "x"])
        for sign, far in st["reach"]:
            ring_send(st, "own", sign, 1, st["own"])
        core_send(st, "own", 0, st["own"])

    for st in streams[:3]:
        begin(st)

    product = g[...].astype(F32) * o[...].astype(F32)
    lane = lax.broadcasted_iota(jnp.int32, (PIECE, 128), 1)
    delta = jnp.zeros((PIECE, 128), F32)
    for h in range(8):
        one = jnp.sum(product[:, h * 64 : (h + 1) * 64], axis=1, keepdims=True)
        delta = jnp.where(lane == h, one, delta)
    own_g[:, 0:512] = g[...]
    own_g[:, 512:640] = delta.astype(BF16)
    begin(streams[3])

    keep = []
    for n, st in enumerate(streams):
        rows = st["rows"](st["pos"], st["ring"], c)
        copy = pltpu.make_async_copy(st["own"], st["full"].at[rows], own_sem.at[n])
        copy.start()
        keep.append(copy)

    for st in streams:
        rows = st["rows"](1 - st["pos"], st["ring"], c)
        post.got(st["slots"]["mate"], st["full"].at[rows])
        for sign, far in st["reach"]:
            ring_send(st, "mate", sign, 1, None)
        core_send(st, "mate", 0, None)

    for d in range(1, 5):
        for s in ("own", "mate"):
            for st in streams:
                for sign, far in st["reach"]:
                    if d > far:
                        continue
                    rows = st["rows"](part_of(st, s), turn(st["ring"], -sign * d), c)
                    post.got(st["slots"][s, sign, d], st["full"].at[rows])
                    if d < far:
                        ring_send(st, s, sign, d + 1, None)
                    core_send(st, s, sign * d, None)

    for st in streams:
        if st["kind"] == "q":
            for (s, shift), slot in st["core"].items():
                rows = st["rows"](part_of(st, s), turn(st["ring"], -shift), 1 - c)
                post.got(slot, st["full"].at[rows])
    for copy in keep:
        copy.wait()
    post.finish()


GATHER_COPIES = 2 * 15 + 2 * (15 + 16)


def gather(q, g, o, k, v):
    shapes = [(1024, 512), (1024, 640), (512, 512), (512, 512)]
    return pl.pallas_call(
        gather_kernel,
        out_shape=[jax.ShapeDtypeStruct(s, BF16) for s in shapes],
        in_specs=[pl.BlockSpec(memory_space=pltpu.VMEM)] * 5,
        out_specs=[pl.BlockSpec(memory_space=pltpu.VMEM)] * 4,
        scratch_shapes=[
            pltpu.VMEM((PIECE, 640), BF16),
            pltpu.SemaphoreType.DMA((4,)),
            pltpu.SemaphoreType.DMA((GATHER_COPIES,)),
            pltpu.SemaphoreType.DMA((GATHER_COPIES,)),
        ],
        compiler_params=pltpu.CompilerParams(collective_id=0, has_side_effects=True),
        name="gather",
    )(q, g, o, k, v)


def scatter_kernel(dq, dk, dv, oq, ok, ov, mine, land, core_land, mate_out, mate_land, send, recv):
    xl, z, xh, y, c = places()
    near = neighbours(xl, z, xh, y, c)
    greet(near)
    post = Post(send, recv)

    order = [4, -4 + 1, 3, -2, 2, -1, 1, 0]
    core_slots = {}
    for n, shift in enumerate(order):
        t = turn(y, shift)
        for a in range(2):
            slot = post.slot()
            core_slots[a, shift] = (slot, n * 2 + a)
            post.put(slot, dq.at[q_rows(a, t, 1 - c)], core_land.at[n * 2 + a], near["qc"])

    def q_part(a, shift):
        slot, n = core_slots[a, shift]
        if shift is not None and (a, shift) not in q_part.seen:
            post.got(slot, core_land.at[n])
            q_part.seen.add((a, shift))
        return dq[q_rows(a, turn(y, shift), c), :].astype(F32) + core_land[n].astype(F32)

    q_part.seen = set()

    def k_part(ref):
        return lambda a, shift: ref[k_rows(a, turn(z, shift)), :].astype(F32)

    chains = []
    count = 0
    for a in range(2):
        for kind, part, reach, ref in (
            ("k", k_part(dk), ((1, 4), (-1, 3)), dk),
            ("k", k_part(dv), ((1, 3), (-1, 4)), dv),
            ("q", q_part, ((1, 4), (-1, 3)) if a == 0 else ((1, 3), (-1, 4)), None),
        ):
            for sign, far in reach:
                chains.append(dict(a=a, kind=kind, part=part, sign=sign, far=far, ref=ref, base=count))
                count += far
    for ch in chains:
        ch["slots"] = [post.slot() for _ in range(ch["far"])]

    for s in range(4):
        for ch in chains:
            far, sign, a = ch["far"], ch["sign"], ch["a"]
            if s >= far:
                continue
            shift = sign * (far - s)
            if shift == -4:
                shift = 4
            here = ch["base"] + s
            way = near[ch["kind"] + ("+" if sign > 0 else "-")]
            if s == 0 and ch["ref"] is not None:
                src = ch["ref"].at[k_rows(a, turn(z, shift))]
            else:
                total = ch["part"](a, shift)
                if s > 0:
                    post.got(ch["slots"][s - 1], land.at[here - 1])
                    total = total + land[here - 1].astype(F32)
                mine[here] = total.astype(BF16)
                src = mine.at[here]
            post.put(ch["slots"][s], src, land.at[here], way)

    mates = [post.slot() for _ in range(3)]
    finals = []
    for n, (kind, pos) in enumerate((("k", xl), ("k", xl), ("q", xh))):
        both = []
        for a in range(2):
            pair = [ch for ch in chains if ch["a"] == a][2 * n : 2 * n + 2]
            total = pair[0]["part"](a, 0)
            for ch in pair:
                last = ch["base"] + ch["far"] - 1
                post.got(ch["slots"][-1], land.at[last])
                total = total + land[last].astype(F32)
            both.append(total)
        here_first = pos == 0
        mate_out[n] = jnp.where(here_first, both[1], both[0]).astype(BF16)
        post.put(mates[n], mate_out.at[n], mate_land.at[n], near[kind + "x"])
        finals.append(jnp.where(here_first, both[0], both[1]))
    for n, out in enumerate((ok, ov, oq)):
        post.got(mates[n], mate_land.at[n])
        out[...] = (finals[n] + mate_land[n].astype(F32)).astype(BF16)
    post.finish()


SCATTER_COPIES = 16 + 42 + 3


def scatter(dq, dk, dv):
    return pl.pallas_call(
        scatter_kernel,
        out_shape=[jax.ShapeDtypeStruct((PIECE, 512), BF16)] * 3,
        in_specs=[pl.BlockSpec(memory_space=pltpu.VMEM)] * 3,
        out_specs=[pl.BlockSpec(memory_space=pltpu.VMEM)] * 3,
        scratch_shapes=[
            pltpu.VMEM((42, PIECE, 512), BF16),
            pltpu.VMEM((42, PIECE, 512), BF16),
            pltpu.VMEM((16, PIECE, 512), BF16),
            pltpu.VMEM((3, PIECE, 512), BF16),
            pltpu.VMEM((3, PIECE, 512), BF16),
            pltpu.SemaphoreType.DMA((SCATTER_COPIES,)),
            pltpu.SemaphoreType.DMA((SCATTER_COPIES,)),
        ],
        compiler_params=pltpu.CompilerParams(collective_id=1, has_side_effects=True),
        name="scatter",
    )(dq, dk, dv)


def attention_kernel(slots, live, q, g, k, v, lse, bits, dq, dk, dv, bias, delta_t, qt, gt, kc, vc, kt, prob, score):
    rows, keys = q.shape[0], k.shape[0]
    scale = 0.125
    bias[...] = jnp.full(bias.shape, NEG, F32)
    bit_of = lax.broadcasted_iota(jnp.int32, (16, 128), 0)

    @pl.loop(0, live[0, 0])
    def _(e):
        slot = slots[0, 0, e]
        across = pl.multiple_of((slot // 4) * 128, 128)
        down = pl.multiple_of(lax.rem(slot, 4) * 128, 128)
        words = bits[e]
        for r in range(8):
            word = jnp.broadcast_to(words[r : r + 1, :], (16, 128))
            edge = jnp.bitwise_and(jnp.right_shift(word, bit_of), 1)
            bias[pl.ds(down + r * 16, 16), pl.ds(across, 128)] = jnp.where(edge == 1, 0.0, NEG)

    delta_t[...] = g[:, 512:640].astype(F32).T

    @pl.loop(0, 4)
    def _(p):
        lanes = pl.ds(pl.multiple_of(p * 128, 128), 128)
        kp = k[:, lanes].astype(F32)
        vp = v[:, lanes].astype(F32)
        qp_t = q[:, lanes].T
        gp_t = g[:, lanes].T
        kt[...] = k[:, lanes].T
        lane = lax.broadcasted_iota(jnp.int32, (keys, 128), 1)
        row = lax.broadcasted_iota(jnp.int32, (16, rows), 0)
        for a in range(2):
            own = (lane < 64) if a == 0 else (lane >= 64)
            free = 64 * (1 - a)
            kc[a] = jnp.where(own, kp, jnp.where(lane < free + 3, 1.0, 0.0) if a == 1 else jnp.where(lane < 67, 1.0, 0.0)).astype(BF16)
            vc[a] = jnp.where(own, vp, jnp.where(lane < free + 1, 1.0, 0.0)).astype(BF16)
            low = lse[pl.ds(2 * p + a, 1), :] * (-8.0)
            first = low.astype(BF16).astype(F32)
            second = (low - first).astype(BF16).astype(F32)
            third = low - first - second
            qt[a] = qp_t
            qt[a, free : free + 16, :] = jnp.where(
                row == 0, first, jnp.where(row == 1, second, jnp.where(row == 2, third, 0.0))
            ).astype(BF16)
            gt[a] = gp_t
            gt[a, free : free + 16, :] = jnp.where(
                row == 0, -delta_t[pl.ds(2 * p + a, 1), :], 0.0
            ).astype(BF16)
        parts = []
        for a in range(2):
            for ib in range(rows // 256):
                for jb in range(keys // 128):
                    js, is_ = slice(jb * 128, jb * 128 + 128), slice(ib * 256, ib * 256 + 256)
                    s = jnp.dot(kc[a, js, :], qt[a, :, is_], preferred_element_type=F32)
                    w = jnp.dot(vc[a, js, :], gt[a, :, is_], preferred_element_type=F32)
                    pr = jnp.exp2(s * (scale * math.log2(math.e)) + bias[js, is_])
                    prob[js, is_] = pr.astype(BF16)
                    score[js, is_] = (pr * w).astype(BF16)
            value_sum = jnp.dot(prob[...], g[:, lanes], preferred_element_type=F32)
            key_sum = jnp.dot(score[...], q[:, lanes], preferred_element_type=F32)
            query_sum = jnp.dot(kt[64 * a : 64 * a + 64, :], score[...], preferred_element_type=F32)
            parts.append((value_sum, key_sum, query_sum))
        dv[:, lanes] = jnp.where(lane < 64, parts[0][0], parts[1][0]).astype(BF16)
        dk[:, lanes] = (jnp.where(lane < 64, parts[0][1], parts[1][1]) * scale).astype(BF16)
        both = jnp.concatenate([parts[0][2], parts[1][2]], axis=0) * scale
        dq[:, lanes] = both.T.astype(BF16)


def attention(slots, live, q, g, k, v, lse, bits):
    rows, keys = q.shape[0], k.shape[0]
    vmem = pl.BlockSpec(memory_space=pltpu.VMEM)
    smem = pl.BlockSpec(memory_space=pltpu.SMEM)
    return pl.pallas_call(
        attention_kernel,
        out_shape=[jax.ShapeDtypeStruct((n, 512), BF16) for n in (rows, keys, keys)],
        in_specs=[smem] * 2 + [vmem] * 6,
        out_specs=[vmem] * 3,
        scratch_shapes=[
            pltpu.VMEM((keys, rows), F32),
            pltpu.VMEM((128, rows), F32),
            pltpu.VMEM((2, 128, rows), BF16),
            pltpu.VMEM((2, 128, rows), BF16),
            pltpu.VMEM((2, keys, 128), BF16),
            pltpu.VMEM((2, keys, 128), BF16),
            pltpu.VMEM((128, keys), BF16),
            pltpu.VMEM((keys, rows), BF16),
            pltpu.VMEM((keys, rows), BF16),
        ],
        compiler_params=pltpu.CompilerParams(vmem_limit_bytes=48 << 20),
        name="attention",
    )(slots, live, q, g, k, v, lse, bits)


def body(queries, keys, values, outputs, grad_out, lse, tile_slot, tile_live, tile_bits):
    q, g, k, v = gather(queries[0], grad_out[0], outputs[0], keys[0], values[0])
    dq, dk, dv = attention(tile_slot, tile_live, q, g, k, v, lse[0], tile_bits[0, 0])
    oq, ok, ov = scatter(dq, dk, dv)
    return oq[None], ok[None], ov[None]


def solution(mesh):
    in_specs = (
        P("row", "col", None),
        P("col", "row", None),
        P("col", "row", None),
        P("row", "col", None),
        P("row", "col", None),
        P("row", None, None),
        P("row", "col", None),
        P("row", "col"),
        P("row", "col", None, None, None),
    )
    out_specs = (P("row", "col", None), P("col", "row", None), P("col", "row", None))
    return jax.shard_map(body, mesh=mesh, in_specs=in_specs, out_specs=out_specs, check_vma=False)
```

```python
import functools
import math

import jax
import jax.numpy as jnp
from jax import lax
from jax.experimental import pallas as pl
from jax.experimental.pallas import tpu as pltpu
from jax.sharding import PartitionSpec as P

MESH = pl.DeviceIdType.MESH
RING = 8
PIECE = 32
NEG = -1e30
F32 = jnp.float32
BF16 = jnp.bfloat16


def places():
    r, col = lax.axis_index("row"), lax.axis_index("col")
    xl, z = r // RING, lax.rem(r, RING)
    c = lax.rem(col, 2)
    y = lax.rem(col // 2, RING)
    xh = col // (2 * RING)
    return xl, z, xh, y, c


def turn(a, d):
    return lax.rem(a + d + RING, RING)


def piece(n):
    return pl.ds(pl.multiple_of(n * PIECE, PIECE), PIECE)


def q_rows(xh, y, c):
    return pl.ds(pl.multiple_of((xh * 16 + y * 2 + c) * PIECE, PIECE), PIECE)


def k_rows(xl, z):
    return pl.ds(pl.multiple_of((xl * 8 + z) * PIECE, PIECE), PIECE)


def neighbours(xl, z, xh, y, c):
    def on_col(xh, y, c):
        return {"col": xh * 16 + y * 2 + c}

    def on_row(xl, z):
        return {"row": xl * 8 + z}

    return {
        "qx": on_col(1 - xh, y, c),
        "qc": on_col(xh, y, 1 - c),
        "q+": on_col(xh, turn(y, 1), c),
        "q-": on_col(xh, turn(y, -1), c),
        "kx": on_row(1 - xl, z),
        "k+": on_row(xl, turn(z, 1)),
        "k-": on_row(xl, turn(z, -1)),
    }


def greet(near):
    barrier = pltpu.get_barrier_semaphore()
    for where in near.values():
        pl.semaphore_signal(barrier, inc=1, device_id=where, device_id_type=MESH)
    pl.semaphore_wait(barrier, len(near))


class Post:
    def __init__(self, send, recv):
        self.send, self.recv, self.count, self.sent = send, recv, 0, []

    def slot(self):
        self.count += 1
        return self.count - 1

    def put(self, slot, src, dst, where):
        copy = pltpu.make_async_remote_copy(
            src_ref=src,
            dst_ref=dst,
            send_sem=self.send.at[slot],
            recv_sem=self.recv.at[slot],
            device_id=where,
            device_id_type=MESH,
        )
        copy.start()
        self.sent.append(copy)

    def got(self, slot, dst):
        pltpu.make_async_copy(dst, dst, self.recv.at[slot]).wait()

    def finish(self):
        for copy in self.sent:
            copy.wait_send()


def fused_kernel(
    q, g, o, k, v, lse_in, slots_in, live_in, bits_in,
    oq, ok, ov,
    qa, ga, ka, va, o_s, lse, bits, slots, live,
    bias, delta_t, qt, gt, kc, vc, kt, prob, score,
    dqp, dkv, core_land, kv_land, kv_mine, q_land, q_mine,
    kv_keep, q_keep, kv_out, kv_mate, q_out, q_mate,
    load_sem, send, recv,
):
    xl, z, xh, y, c = places()
    near = neighbours(xl, z, xh, y, c)
    rows, keys = qa.shape[1], ka.shape[1]
    scale = 0.125

    my_q, my_k = q_rows(xh, y, c), k_rows(xl, z)
    loads = {}

    def load(name, pairs):
        made = []
        for src, dst in pairs:
            copy = pltpu.make_async_copy(src, dst, load_sem.at[load.count])
            load.count += 1
            copy.start()
            made.append(copy)
        loads[name] = made

    def loaded(*names):
        for name in names:
            for copy in loads[name]:
                copy.wait()

    load.count = 0
    for name, src, full, where in (("k", k, ka, my_k), ("q", q, qa, my_q), ("v", v, va, my_k), ("g", g, ga, my_q)):
        load(name, [(src.at[:, p * 128 : p * 128 + 128], full.at[p, where, :]) for p in range(4)])
    load("o", [(o.at[:, p * 128 : p * 128 + 128], o_s.at[p]) for p in range(4)])
    load("tables", [(slots_in, slots), (live_in, live), (bits_in, bits)])
    load("lse", [(lse_in, lse)])

    greet(near)
    post = Post(send, recv)

    streams = {}
    for name, kind, full, place, reach in (
        ("k", "k", ka, (xl, z), ((1, 4), (-1, 3))),
        ("q", "q", qa, (xh, y), ((1, 4), (-1, 3))),
        ("v", "k", va, (xl, z), ((1, 3), (-1, 4))),
        ("g", "q", ga, (xh, y), ((1, 3), (-1, 4))),
    ):
        st = dict(kind=kind, full=full, pos=place[0], ring=place[1], reach=reach, slots={}, core={})
        st["rows"] = q_rows if kind == "q" else (lambda x, t, core: k_rows(x, t))
        st["mate"] = post.slot()
        for s in range(2):
            shifts = [0]
            for sign, far in reach:
                for d in range(1, far + 1):
                    st["slots"][s, sign, d] = post.slot()
                    shifts.append(sign * d)
            if kind == "q":
                for shift in shifts:
                    st["core"][s, shift] = post.slot()
        streams[name] = st

    def piece_of(st, s, shift, core):
        pos = st["pos"] if s == 0 else 1 - st["pos"]
        return st["full"].at[:, st["rows"](pos, turn(st["ring"], -shift), core), :]

    def ring_send(st, s, sign, d):
        ref = piece_of(st, s, sign * (d - 1), c)
        post.put(st["slots"][s, sign, d], ref, ref, near[st["kind"] + ("+" if sign > 0 else "-")])

    def core_send(st, s, shift):
        if st["kind"] == "q":
            ref = piece_of(st, s, shift, c)
            post.put(st["core"][s, shift], ref, ref, near["qc"])

    def begin(st):
        ref = piece_of(st, 0, 0, c)
        post.put(st["mate"], ref, ref, near[st["kind"] + "x"])
        for sign, _ in st["reach"]:
            ring_send(st, 0, sign, 1)
        core_send(st, 0, 0)

    def relay(st, s, d):
        for sign, far in st["reach"]:
            if d <= far:
                post.got(st["slots"][s, sign, d], piece_of(st, s, sign * d, c))
                if d < far:
                    ring_send(st, s, sign, d + 1)
                core_send(st, s, sign * d)

    def relay_mate(st):
        post.got(st["mate"], piece_of(st, 1, 0, c))
        for sign, _ in st["reach"]:
            ring_send(st, 1, sign, 1)
        core_send(st, 1, 0)

    for name in ("k", "q", "v"):
        loaded(name)
        begin(streams[name])
    loaded("g", "o")
    lane = lax.broadcasted_iota(jnp.int32, (PIECE, 128), 1)
    delta = jnp.zeros((PIECE, 128), F32)
    for p in range(4):
        product = ga[p, my_q, :].astype(F32) * o_s[p].astype(F32)
        for a in range(2):
            one = jnp.sum(product[:, a * 64 : a * 64 + 64], axis=1, keepdims=True)
            delta = jnp.where(lane == 2 * p + a, one, delta)
    ga[4, my_q, :] = delta.astype(BF16)
    begin(streams["g"])

    loaded("tables")
    bit_of = lax.broadcasted_iota(jnp.int32, (16, 128), 0)
    listed = live[0, 0]

    @pl.loop(0, 32)
    def _(t):
        entry, valid = jnp.int32(0), jnp.int32(0)
        for e in range(24):
            hit = jnp.logical_and(slots[0, 0, e] == t, e < listed)
            entry = jnp.where(hit, jnp.int32(e), entry)
            valid = jnp.where(hit, jnp.int32(1), valid)
        words = bits[entry] * valid
        across = pl.multiple_of((t // 4) * 128, 128)
        down = pl.multiple_of(lax.rem(t, 4) * 128, 128)
        for r in range(8):
            word = jnp.broadcast_to(words[r : r + 1, :], (16, 128))
            edge = jnp.bitwise_and(jnp.right_shift(word, bit_of), 1)
            bias[pl.ds(down + r * 16, 16), pl.ds(across, 128)] = jnp.where(edge == 1, 0.0, NEG)

    names = ("k", "q", "v", "g")
    for d in range(1, 6):
        if d <= 4:
            for n in names:
                relay(streams[n], 0, d)
        for n in names:
            if d == 1:
                relay_mate(streams[n])
            else:
                relay(streams[n], 1, d - 1)
    for n in ("q", "g"):
        st = streams[n]
        for (s, shift), slot in st["core"].items():
            post.got(slot, piece_of(st, s, shift, 1 - c))
    loaded("lse")

    for p in range(4):
        pass
    book = [
        dict(core=post.slot(), kv=[[post.slot() for _ in range(4)] for _ in range(2)],
             q=[[post.slot() for _ in range(4)] for _ in range(2)], kvm=post.slot(), qm=post.slot())
        for _ in range(4)
    ]
    signs = ((0, 1), (1, -1))

    def kv_send(p, si, s, src, dst):
        post.put(book[p]["kv"][si][s], src, dst, near["k+" if si == 0 else "k-"])

    def scatter_start(p):
        post.put(book[p]["core"], dqp.at[p, :, :, 1 - c], core_land.at[p], near["qc"])
        far = piece(turn(z, 4))
        for si, _ in signs:
            half = slice(2 * si, 2 * si + 2)
            kv_send(p, si, 0, dkv.at[p, half, far, :], kv_land.at[p, si, 0, half])

    def kv_step(p, s):
        for si, sign in signs:
            half = slice(2 * si, 2 * si + 2)
            mine = piece(turn(z, sign * (4 - s)))
            if s == 1:
                post.got(book[p]["kv"][si][0], kv_land.at[p, si, 0, half])
                kv_mine[p, si, 1] = dkv[p, :, mine, :]
                kv_mine[p, si, 1, half] = (
                    dkv[p, half, mine, :].astype(F32) + kv_land[p, si, 0, half].astype(F32)
                ).astype(BF16)
            else:
                post.got(book[p]["kv"][si][s - 1], kv_land.at[p, si, s - 1])
                kv_mine[p, si, s] = (
                    dkv[p, :, mine, :].astype(F32) + kv_land[p, si, s - 1].astype(F32)
                ).astype(BF16)
            kv_send(p, si, s, kv_mine.at[p, si, s], kv_land.at[p, si, s])

    def q_own(p, t):
        return dqp[p, :, t, c].astype(F32) + core_land[p, :, t].astype(F32)

    def q_step(p, s):
        if s == 0:
            post.got(book[p]["core"], core_land.at[p])
        for si, sign in signs:
            t = turn(y, sign * (4 - s))
            way = near["q+" if si == 0 else "q-"]
            if s == 0:
                total = dqp[p, si, t, c].astype(F32) + core_land[p, si, t].astype(F32)
                q_mine[p, si, 0, si] = total.astype(BF16)
                post.put(book[p]["q"][si][0], q_mine.at[p, si, 0, si], q_land.at[p, si, 0, si], way)
                continue
            total = q_own(p, t)
            if s == 1:
                post.got(book[p]["q"][si][0], q_land.at[p, si, 0, si])
                q_mine[p, si, 1, 1 - si] = total[1 - si].astype(BF16)
                q_mine[p, si, 1, si] = (total[si] + q_land[p, si, 0, si].astype(F32)).astype(BF16)
            else:
                post.got(book[p]["q"][si][s - 1], q_land.at[p, si, s - 1])
                q_mine[p, si, s] = (total + q_land[p, si, s - 1].astype(F32)).astype(BF16)
            post.put(book[p]["q"][si][s], q_mine.at[p, si, s], q_land.at[p, si, s], way)

    def kv_final(p):
        total = dkv[p, :, piece(z), :].astype(F32)
        for si, _ in signs:
            post.got(book[p]["kv"][si][3], kv_land.at[p, si, 3])
            total = total + kv_land[p, si, 3].astype(F32)
        for n in range(2):
            kv_keep[p, n] = jnp.where(xl == 0, total[2 * n], total[2 * n + 1])
            kv_out[p, n] = jnp.where(xl == 0, total[2 * n + 1], total[2 * n]).astype(BF16)
        post.put(book[p]["kvm"], kv_out.at[p], kv_mate.at[p], near["kx"])

    def q_final(p):
        total = q_own(p, y)
        for si, _ in signs:
            post.got(book[p]["q"][si][3], q_land.at[p, si, 3])
            total = total + q_land[p, si, 3].astype(F32)
        q_keep[p] = jnp.where(xh == 0, total[0], total[1])
        q_out[p] = jnp.where(xh == 0, total[1], total[0]).astype(BF16)
        post.put(book[p]["qm"], q_out.at[p], q_mate.at[p], near["qx"])

    def kv_done(p):
        post.got(book[p]["kvm"], kv_mate.at[p])
        for n, out in enumerate((ok, ov)):
            out[:, p * 128 : p * 128 + 128] = (kv_keep[p, n] + kv_mate[p, n].astype(F32)).astype(BF16)

    def q_done(p):
        post.got(book[p]["qm"], q_mate.at[p])
        oq[:, p * 128 : p * 128 + 128] = (q_keep[p] + q_mate[p].astype(F32)).astype(BF16)

    turns = {
        "kv": [functools.partial(kv_step, s=s) for s in range(1, 4)] + [kv_final, kv_done],
        "q": [functools.partial(q_step, s=s) for s in range(4)] + [q_final, q_done],
    }
    at = {(kind, p): 0 for kind in turns for p in range(4)}

    def advance(kind, p):
        n = at[kind, p]
        if 0 <= p and n < len(turns[kind]):
            turns[kind][n](p)
            at[kind, p] = n + 1
            return True
        return False

    delta_t[...] = ga[4].astype(F32).T
    lane = lax.broadcasted_iota(jnp.int32, (keys, 128), 1)
    row = lax.broadcasted_iota(jnp.int32, (16, rows), 0)
    for p in range(4):
        kp = ka[p].astype(F32)
        vp = va[p].astype(F32)
        qp_t = qa[p].T
        gp_t = ga[p].T
        kt[...] = ka[p].T
        for a in range(2):
            own = (lane < 64) if a == 0 else (lane >= 64)
            free = 64 * (1 - a)
            kc[a] = jnp.where(own, kp, jnp.where(lane < free + 3, 1.0, 0.0)).astype(BF16)
            vc[a] = jnp.where(own, vp, jnp.where(lane < free + 1, 1.0, 0.0)).astype(BF16)
            low = lse[2 * p + a : 2 * p + a + 1, :] * (-8.0)
            first = low.astype(BF16).astype(F32)
            second = (low - first).astype(BF16).astype(F32)
            third = low - first - second
            qt[a] = qp_t
            qt[a, free : free + 16, :] = jnp.where(
                row == 0, first, jnp.where(row == 1, second, jnp.where(row == 2, third, 0.0))
            ).astype(BF16)
            gt[a] = gp_t
            gt[a, free : free + 16, :] = jnp.where(
                row == 0, -delta_t[2 * p + a : 2 * p + a + 1, :], 0.0
            ).astype(BF16)
        parts = []
        for a in range(2):
            for ib in range(rows // 256):
                for jb in range(keys // 128):
                    js, is_ = slice(jb * 128, jb * 128 + 128), slice(ib * 256, ib * 256 + 256)
                    s = jnp.dot(kc[a, js, :], qt[a, :, is_], preferred_element_type=F32)
                    w = jnp.dot(vc[a, js, :], gt[a, :, is_], preferred_element_type=F32)
                    pr = jnp.exp2(s * (scale * math.log2(math.e)) + bias[js, is_])
                    prob[js, is_] = pr.astype(BF16)
                    score[js, is_] = (pr * w).astype(BF16)
            value_sum = jnp.dot(prob[...], ga[p], preferred_element_type=F32)
            key_sum = jnp.dot(score[...], qa[p], preferred_element_type=F32)
            query_sum = jnp.dot(kt[64 * a : 64 * a + 64, :], score[...], preferred_element_type=F32)
            parts.append((value_sum, key_sum, query_sum))
            if a == 0:
                for back in range(1, 4):
                    if p >= back:
                        advance("q", p - back)
        dkv[p, 0:2] = (jnp.where(lane < 64, parts[0][1], parts[1][1]) * scale).astype(BF16).reshape(2, 256, 128)
        dkv[p, 2:4] = jnp.where(lane < 64, parts[0][0], parts[1][0]).astype(BF16).reshape(2, 256, 128)
        both = jnp.concatenate([parts[0][2], parts[1][2]], axis=0) * scale
        dqp[p] = both.T.astype(BF16).reshape(2, 8, 2, PIECE, 128)
        scatter_start(p)
        for back in range(1, 4):
            if p >= back:
                advance("kv", p - back)
    busy = True
    while busy:
        busy = False
        for p in range(4):
            for kind in ("kv", "q"):
                busy = advance(kind, p) or busy
    post.finish()


COPIES = 2 * 15 + 2 * (15 + 16) + 4 * 19


def fused(q, g, o, k, v, lse, slots, live, bits):
    vmem = pl.BlockSpec(memory_space=pltpu.VMEM)
    hbm = pl.BlockSpec(memory_space=pl.ANY)
    rows, keys = 1024, 512
    return pl.pallas_call(
        fused_kernel,
        out_shape=[jax.ShapeDtypeStruct((PIECE, 512), BF16)] * 3,
        in_specs=[hbm] * 9,
        out_specs=[vmem] * 3,
        scratch_shapes=[
            pltpu.VMEM((4, rows, 128), BF16),
            pltpu.VMEM((5, rows, 128), BF16),
            pltpu.VMEM((4, keys, 128), BF16),
            pltpu.VMEM((4, keys, 128), BF16),
            pltpu.VMEM((4, PIECE, 128), BF16),
            pltpu.VMEM(lse.shape, F32),
            pltpu.VMEM(bits.shape, jnp.int32),
            pltpu.SMEM(slots.shape, jnp.int32),
            pltpu.SMEM(live.shape, jnp.int32),
            pltpu.VMEM((keys, rows), F32),
            pltpu.VMEM((128, rows), F32),
            pltpu.VMEM((2, 128, rows), BF16),
            pltpu.VMEM((2, 128, rows), BF16),
            pltpu.VMEM((2, keys, 128), BF16),
            pltpu.VMEM((2, keys, 128), BF16),
            pltpu.VMEM((128, keys), BF16),
            pltpu.VMEM((keys, rows), BF16),
            pltpu.VMEM((keys, rows), BF16),
            pltpu.VMEM((4, 2, 8, 2, PIECE, 128), BF16),
            pltpu.VMEM((4, 4, 256, 128), BF16),
            pltpu.VMEM((4, 2, 8, PIECE, 128), BF16),
            pltpu.VMEM((4, 2, 4, 4, PIECE, 128), BF16),
            pltpu.VMEM((4, 2, 4, 4, PIECE, 128), BF16),
            pltpu.VMEM((4, 2, 4, 2, PIECE, 128), BF16),
            pltpu.VMEM((4, 2, 4, 2, PIECE, 128), BF16),
            pltpu.VMEM((4, 2, PIECE, 128), F32),
            pltpu.VMEM((4, PIECE, 128), F32),
            pltpu.VMEM((4, 2, PIECE, 128), BF16),
            pltpu.VMEM((4, 2, PIECE, 128), BF16),
            pltpu.VMEM((4, PIECE, 128), BF16),
            pltpu.VMEM((4, PIECE, 128), BF16),
            pltpu.SemaphoreType.DMA((24,)),
            pltpu.SemaphoreType.DMA((COPIES,)),
            pltpu.SemaphoreType.DMA((COPIES,)),
        ],
        compiler_params=pltpu.CompilerParams(
            collective_id=0, has_side_effects=True, vmem_limit_bytes=56 << 20
        ),
        name="fused",
    )(q, g, o, k, v, lse, slots, live, bits)


def body(queries, keys, values, outputs, grad_out, lse, tile_slot, tile_live, tile_bits):
    oq, ok, ov = fused(
        queries[0], grad_out[0], outputs[0], keys[0], values[0], lse[0], tile_slot, tile_live, tile_bits[0, 0]
    )
    return oq[None], ok[None], ov[None]


def solution(mesh):
    in_specs = (
        P("row", "col", None),
        P("col", "row", None),
        P("col", "row", None),
        P("row", "col", None),
        P("row", "col", None),
        P("row", None, None),
        P("row", "col", None),
        P("row", "col"),
        P("row", "col", None, None, None),
    )
    out_specs = (P("row", "col", None), P("col", "row", None), P("col", "row", None))
    return jax.shard_map(body, mesh=mesh, in_specs=in_specs, out_specs=out_specs, check_vma=False)
```

```python
import functools
import math

import jax
import jax.numpy as jnp
from jax import lax
from jax.experimental import pallas as pl
from jax.experimental.pallas import tpu as pltpu
from jax.sharding import PartitionSpec as P

MESH = pl.DeviceIdType.MESH
RING = 8
PIECE = 32
NEG = -1e30
F32 = jnp.float32
BF16 = jnp.bfloat16


def places():
    r, col = lax.axis_index("row"), lax.axis_index("col")
    xl, z = r // RING, lax.rem(r, RING)
    c = lax.rem(col, 2)
    y = lax.rem(col // 2, RING)
    xh = col // (2 * RING)
    return xl, z, xh, y, c


def turn(a, d):
    return lax.rem(a + d + RING, RING)


def piece(n):
    return pl.ds(pl.multiple_of(n * PIECE, PIECE), PIECE)


def q_rows(xh, y, c):
    return pl.ds(pl.multiple_of((xh * 16 + y * 2 + c) * PIECE, PIECE), PIECE)


def k_rows(xl, z):
    return pl.ds(pl.multiple_of((xl * 8 + z) * PIECE, PIECE), PIECE)


CHAIN = {1: 0, 2: 1, 3: 2, 4: 3, -1: 0, -2: -1, -3: -2}
DEEP = {1: 0, 2: 0, 3: 2, 4: 3, -1: 0, -2: -1, -3: -2}
FLAT = {1: 0, 2: 1, 3: 0, 4: 3, -1: 0, -2: 0, -3: -2}


def mirror(tree):
    return {-child: -parent for child, parent in tree.items()}


def neighbours(xl, z, xh, y, c):
    near = {"core": {"col": xh * 16 + y * 2 + 1 - c}}
    for far in range(-3, 4):
        for other in range(2):
            if far == 0 and other == 0:
                continue
            x = 1 - xh if other else xh
            near["q", other, far] = {"col": x * 16 + turn(y, far) * 2 + c}
            x = 1 - xl if other else xl
            near["k", other, far] = {"row": x * 8 + turn(z, far)}
    return near


def greet(near):
    barrier = pltpu.get_barrier_semaphore()
    for where in near.values():
        pl.semaphore_signal(barrier, inc=1, device_id=where, device_id_type=MESH)
    pl.semaphore_wait(barrier, len(near))


class Post:
    def __init__(self, send, recv):
        self.send, self.recv, self.count, self.sent = send, recv, 0, []

    def slot(self):
        self.count += 1
        return self.count - 1

    def put(self, slot, src, dst, where):
        copy = pltpu.make_async_remote_copy(
            src_ref=src,
            dst_ref=dst,
            send_sem=self.send.at[slot],
            recv_sem=self.recv.at[slot],
            device_id=where,
            device_id_type=MESH,
        )
        copy.start()
        self.sent.append(copy)

    def got(self, slot, dst):
        pltpu.make_async_copy(dst, dst, self.recv.at[slot]).wait()

    def finish(self):
        for copy in self.sent:
            copy.wait_send()


OWN_TREE, MATE_TREE = CHAIN, FLAT


def fused_kernel(
    q, g, o, k, v, lse_in, slots_in, live_in, bits_in,
    oq, ok, ov,
    qa, ga, ka, va, o_s, lse, bits, slots, live,
    bias, delta_t, qt, gt, kc, vc, kt, prob, score,
    dqp, dkv, core_land, kv_leaf, kv_mine, kv_root, q_leaf, q_mine, q_root,
    load_sem, send, recv,
):
    xl, z, xh, y, c = places()
    near = neighbours(xl, z, xh, y, c)
    rows, keys = qa.shape[1], ka.shape[1]
    scale = 0.125

    my_q, my_k = q_rows(xh, y, c), k_rows(xl, z)
    loads = {}

    def load(name, pairs):
        made = []
        for src, dst in pairs:
            copy = pltpu.make_async_copy(src, dst, load_sem.at[load.count])
            load.count += 1
            copy.start()
            made.append(copy)
        loads[name] = made

    def loaded(*names):
        for name in names:
            for copy in loads[name]:
                copy.wait()

    load.count = 0
    for name, src, full, where in (("k", k, ka, my_k), ("q", q, qa, my_q), ("v", v, va, my_k), ("g", g, ga, my_q)):
        load(name, [(src.at[:, p * 128 : p * 128 + 128], full.at[p, where, :]) for p in range(4)])
    load("o", [(o.at[:, p * 128 : p * 128 + 128], o_s.at[p]) for p in range(4)])
    load("tables", [(slots_in, slots), (live_in, live), (bits_in, bits)])
    load("lse", [(lse_in, lse)])

    greet(near)
    post = Post(send, recv)

    streams = {}
    for name, kind, full, place, flip in (
        ("k", "k", ka, (xl, z), False),
        ("q", "q", qa, (xh, y), False),
        ("v", "k", va, (xl, z), True),
        ("g", "q", ga, (xh, y), True),
    ):
        trees = [mirror(t) if flip else t for t in (OWN_TREE, MATE_TREE)]
        st = dict(kind=kind, full=full, pos=place[0], ring=place[1], trees=trees, slots={}, core={}, mate=post.slot())
        st["rows"] = q_rows if kind == "q" else (lambda x, t, core: k_rows(x, t))
        for s in range(2):
            for d in trees[s]:
                st["slots"][s, d] = post.slot()
            if kind == "q":
                for d in (0, *trees[s]):
                    st["core"][s, d] = post.slot()
        streams[name] = st

    def piece_of(st, s, shift, core):
        pos = st["pos"] if s == 0 else 1 - st["pos"]
        return st["full"].at[:, st["rows"](pos, turn(st["ring"], -shift), core), :]

    def pass_on(st, s, d):
        ref = piece_of(st, s, d, c)
        for child, parent in sorted(st["trees"][s].items(), key=lambda e: -abs(e[0] - e[1])):
            if parent == d:
                post.put(st["slots"][s, child], ref, ref, near[st["kind"], 0, child - parent])
        if st["kind"] == "q":
            post.put(st["core"][s, d], ref, ref, near["core"])

    def begin(st):
        ref = piece_of(st, 0, 0, c)
        post.put(st["mate"], ref, ref, near[st["kind"], 1, 0])
        pass_on(st, 0, 0)

    def arrive(st, s, d):
        if (s, d) == (1, 0):
            post.got(st["mate"], piece_of(st, 1, 0, c))
        else:
            post.got(st["slots"][s, d], piece_of(st, s, d, c))
        pass_on(st, s, d)

    def arrivals():
        found = []
        for n, name in enumerate(("k", "q", "v", "g")):
            st = streams[name]
            for s in range(2):
                first = 0.0 if s == 0 else (2.6 if st["kind"] == "k" else 3.6)
                first += 0.4 * n + (1.5 if name == "g" else 0.0)
                if s == 1:
                    found.append((first, name, 1, 0))
                for d in st["trees"][s]:
                    when, at_d = first, d
                    while at_d != 0:
                        up = st["trees"][s][at_d]
                        when += 2.9 + 0.6 * (abs(at_d - up) - 1)
                        at_d = up
                    found.append((when, name, s, d))
        return sorted(found)

    for name in ("k", "q", "v"):
        loaded(name)
        begin(streams[name])
    loaded("g", "o")
    lane = lax.broadcasted_iota(jnp.int32, (PIECE, 128), 1)
    delta = jnp.zeros((PIECE, 128), F32)
    for p in range(4):
        product = ga[p, my_q, :].astype(F32) * o_s[p].astype(F32)
        for a in range(2):
            one = jnp.sum(product[:, a * 64 : a * 64 + 64], axis=1, keepdims=True)
            delta = jnp.where(lane == 2 * p + a, one, delta)
    ga[4, my_q, :] = delta.astype(BF16)
    begin(streams["g"])

    loaded("tables")
    bit_of = lax.broadcasted_iota(jnp.int32, (16, 128), 0)
    listed = live[0, 0]

    @pl.loop(0, 32)
    def _(t):
        entry, valid = jnp.int32(0), jnp.int32(0)
        for e in range(24):
            hit = jnp.logical_and(slots[0, 0, e] == t, e < listed)
            entry = jnp.where(hit, jnp.int32(e), entry)
            valid = jnp.where(hit, jnp.int32(1), valid)
        words = bits[entry] * valid
        across = pl.multiple_of((t // 4) * 128, 128)
        down = pl.multiple_of(lax.rem(t, 4) * 128, 128)
        for r in range(8):
            word = jnp.broadcast_to(words[r : r + 1, :], (16, 128))
            edge = jnp.bitwise_and(jnp.right_shift(word, bit_of), 1)
            bias[pl.ds(down + r * 16, 16), pl.ds(across, 128)] = jnp.where(edge == 1, 0.0, NEG)

    for _, name, s, d in arrivals():
        arrive(streams[name], s, d)
    for n in ("q", "g"):
        st = streams[n]
        for (s, shift), slot in st["core"].items():
            post.got(slot, piece_of(st, s, shift, 1 - c))
    loaded("lse")

    trees = (FLAT, mirror(FLAT))
    leaves = [[d for d in t if d not in t.values() and t[d] != 0] for t in trees]
    tops = [[d for d in t if t[d] == 0] for t in trees]
    book = []
    for p in range(4):
        entry = dict(core=post.slot())
        for kind in ("kv", "q"):
            for n in range(2):
                for d in leaves[n]:
                    entry[kind, n, "leaf", d] = post.slot()
                for b in range(2) if kind == "kv" else (n,):
                    for d in tops[n] + ([0] if b == 1 else []):
                        entry[kind, n, b, d] = post.slot()
        book.append(entry)

    def child_of(n, d):
        found = [e for e, up in trees[n].items() if up == d]
        return found[0] if found else None

    def kv_top(p, n, b, d, src):
        dst = kv_root.at[p, n, b, tops[n].index(d) if d else 4]
        post.put(book[p]["kv", n, b, d], src, dst, near["k", b, -d])

    def kv_side(b):
        return xl if b == 0 else 1 - xl

    def scatter_start(p):
        post.put(book[p]["core"], dqp.at[p, :, :, 1 - c], core_land.at[p], near["core"])
        for n in range(2):
            for i, d in enumerate(leaves[n]):
                src = dkv.at[p, 2 * n : 2 * n + 2, piece(turn(z, -d)), :]
                post.put(book[p]["kv", n, "leaf", d], src, kv_leaf.at[p, n, i], near["k", 0, trees[n][d] - d])
            for d in tops[n]:
                if child_of(n, d) is None:
                    for b in range(2):
                        kv_top(p, n, b, d, dkv.at[p, 2 * n + kv_side(b), piece(turn(z, -d)), :])
            kv_top(p, n, 1, 0, dkv.at[p, 2 * n + kv_side(1), piece(z), :])

    def kv_middle(p):
        for n in range(2):
            for j, d in enumerate(tops[n]):
                e = child_of(n, d)
                if e is None:
                    continue
                i = leaves[n].index(e)
                post.got(book[p]["kv", n, "leaf", e], kv_leaf.at[p, n, i])
                own = dkv[p, 2 * n : 2 * n + 2, piece(turn(z, -d)), :].astype(F32)
                kv_mine[p, n, j] = (own + kv_leaf[p, n, i].astype(F32)).astype(BF16)
                for b in range(2):
                    kv_top(p, n, b, d, kv_mine.at[p, n, j, kv_side(b)])

    def kv_final(p):
        for n, out in enumerate((ok, ov)):
            total = dkv[p, 2 * n + xl, piece(z), :].astype(F32)
            for b in range(2):
                for d in tops[n] + ([0] if b == 1 else []):
                    i = tops[n].index(d) if d else 4
                    post.got(book[p]["kv", n, b, d], kv_root.at[p, n, b, i])
                    total = total + kv_root[p, n, b, i].astype(F32)
            out[:, p * 128 : p * 128 + 128] = total.astype(BF16)

    def q_own(p, b, t):
        side = xh if b == 0 else 1 - xh
        return dqp[p, side, t, c].astype(F32) + core_land[p, side, t].astype(F32)

    def q_put(p, b, d, total):
        i = (leaves[b] + tops[b] + [0]).index(d)
        q_mine[p, b, i] = total.astype(BF16)
        if d in leaves[b]:
            slot, dst = book[p]["q", b, "leaf", d], q_leaf.at[p, b, i]
            post.put(slot, q_mine.at[p, b, i], dst, near["q", 0, trees[b][d] - d])
        else:
            dst = q_root.at[p, b, i - len(leaves[b])]
            post.put(book[p]["q", b, b, d], q_mine.at[p, b, i], dst, near["q", b, -d])

    def q_first(p):
        post.got(book[p]["core"], core_land.at[p])
        for b in range(2):
            for d in leaves[b] + [d for d in tops[b] if child_of(b, d) is None]:
                q_put(p, b, d, q_own(p, b, turn(y, -d)))
        q_put(p, 1, 0, q_own(p, 1, y))

    def q_middle(p):
        for b in range(2):
            for d in tops[b]:
                e = child_of(b, d)
                if e is None:
                    continue
                i = leaves[b].index(e)
                post.got(book[p]["q", b, "leaf", e], q_leaf.at[p, b, i])
                q_put(p, b, d, q_own(p, b, turn(y, -d)) + q_leaf[p, b, i].astype(F32))

    def q_final(p):
        total = q_own(p, 0, y)
        for b in range(2):
            for d in tops[b] + ([0] if b == 1 else []):
                i = tops[b].index(d) if d else 4
                post.got(book[p]["q", b, b, d], q_root.at[p, b, i])
                total = total + q_root[p, b, i].astype(F32)
        oq[:, p * 128 : p * 128 + 128] = total.astype(BF16)

    delta_t[...] = ga[4].astype(F32).T
    lane = lax.broadcasted_iota(jnp.int32, (keys, 128), 1)
    row = lax.broadcasted_iota(jnp.int32, (16, rows), 0)
    for p in range(4):
        kp = ka[p].astype(F32)
        vp = va[p].astype(F32)
        qp_t = qa[p].T
        gp_t = ga[p].T
        kt[...] = ka[p].T
        for a in range(2):
            own = (lane < 64) if a == 0 else (lane >= 64)
            free = 64 * (1 - a)
            kc[a] = jnp.where(own, kp, jnp.where(lane < free + 3, 1.0, 0.0)).astype(BF16)
            vc[a] = jnp.where(own, vp, jnp.where(lane < free + 1, 1.0, 0.0)).astype(BF16)
            low = lse[2 * p + a : 2 * p + a + 1, :] * (-8.0)
            first = low.astype(BF16).astype(F32)
            second = (low - first).astype(BF16).astype(F32)
            third = low - first - second
            qt[a] = qp_t
            qt[a, free : free + 16, :] = jnp.where(
                row == 0, first, jnp.where(row == 1, second, jnp.where(row == 2, third, 0.0))
            ).astype(BF16)
            gt[a] = gp_t
            gt[a, free : free + 16, :] = jnp.where(
                row == 0, -delta_t[2 * p + a : 2 * p + a + 1, :], 0.0
            ).astype(BF16)
        parts = []
        for a in range(2):
            for ib in range(rows // 256):
                for jb in range(keys // 128):
                    js, is_ = slice(jb * 128, jb * 128 + 128), slice(ib * 256, ib * 256 + 256)
                    s = jnp.dot(kc[a, js, :], qt[a, :, is_], preferred_element_type=F32)
                    w = jnp.dot(vc[a, js, :], gt[a, :, is_], preferred_element_type=F32)
                    pr = jnp.exp2(s * (scale * math.log2(math.e)) + bias[js, is_])
                    prob[js, is_] = pr.astype(BF16)
                    score[js, is_] = (pr * w).astype(BF16)
            value_sum = jnp.dot(prob[...], ga[p], preferred_element_type=F32)
            key_sum = jnp.dot(score[...], qa[p], preferred_element_type=F32)
            query_sum = jnp.dot(kt[64 * a : 64 * a + 64, :], score[...], preferred_element_type=F32)
            parts.append((value_sum, key_sum, query_sum))
            if a == 0:
                if p >= 1:
                    q_first(p - 1)
                if p >= 2:
                    kv_middle(p - 2)
        dkv[p, 0:2] = (jnp.where(lane < 64, parts[0][1], parts[1][1]) * scale).astype(BF16).reshape(2, 256, 128)
        dkv[p, 2:4] = jnp.where(lane < 64, parts[0][0], parts[1][0]).astype(BF16).reshape(2, 256, 128)
        both = jnp.concatenate([parts[0][2], parts[1][2]], axis=0) * scale
        dqp[p] = both.T.astype(BF16).reshape(2, 8, 2, PIECE, 128)
        scatter_start(p)
        if p >= 2:
            q_middle(p - 2)
        if p >= 3:
            kv_final(p - 3)
    q_first(3)
    kv_middle(2)
    q_middle(2)
    kv_middle(3)
    q_middle(3)
    for p in range(4):
        if p > 0:
            kv_final(p)
        q_final(p)
    post.finish()


COPIES = 2 * 15 + 2 * (15 + 16) + 4 * 40


def fused(q, g, o, k, v, lse, slots, live, bits):
    vmem = pl.BlockSpec(memory_space=pltpu.VMEM)
    hbm = pl.BlockSpec(memory_space=pl.ANY)
    rows, keys = 1024, 512
    return pl.pallas_call(
        fused_kernel,
        out_shape=[jax.ShapeDtypeStruct((PIECE, 512), BF16)] * 3,
        in_specs=[hbm] * 9,
        out_specs=[vmem] * 3,
        scratch_shapes=[
            pltpu.VMEM((4, rows, 128), BF16),
            pltpu.VMEM((5, rows, 128), BF16),
            pltpu.VMEM((4, keys, 128), BF16),
            pltpu.VMEM((4, keys, 128), BF16),
            pltpu.VMEM((4, PIECE, 128), BF16),
            pltpu.VMEM(lse.shape, F32),
            pltpu.VMEM(bits.shape, jnp.int32),
            pltpu.SMEM(slots.shape, jnp.int32),
            pltpu.SMEM(live.shape, jnp.int32),
            pltpu.VMEM((keys, rows), F32),
            pltpu.VMEM((128, rows), F32),
            pltpu.VMEM((2, 128, rows), BF16),
            pltpu.VMEM((2, 128, rows), BF16),
            pltpu.VMEM((2, keys, 128), BF16),
            pltpu.VMEM((2, keys, 128), BF16),
            pltpu.VMEM((128, keys), BF16),
            pltpu.VMEM((keys, rows), BF16),
            pltpu.VMEM((keys, rows), BF16),
            pltpu.VMEM((4, 2, 8, 2, PIECE, 128), BF16),
            pltpu.VMEM((4, 4, 256, 128), BF16),
            pltpu.VMEM((4, 2, 8, PIECE, 128), BF16),
            pltpu.VMEM((4, 2, 3, 2, PIECE, 128), BF16),
            pltpu.VMEM((4, 2, 4, 2, PIECE, 128), BF16),
            pltpu.VMEM((4, 2, 2, 5, PIECE, 128), BF16),
            pltpu.VMEM((4, 2, 3, PIECE, 128), BF16),
            pltpu.VMEM((4, 2, 8, PIECE, 128), BF16),
            pltpu.VMEM((4, 2, 5, PIECE, 128), BF16),
            pltpu.SemaphoreType.DMA((24,)),
            pltpu.SemaphoreType.DMA((COPIES,)),
            pltpu.SemaphoreType.DMA((COPIES,)),
        ],
        compiler_params=pltpu.CompilerParams(
            collective_id=0, has_side_effects=True, vmem_limit_bytes=56 << 20
        ),
        name="fused",
    )(q, g, o, k, v, lse, slots, live, bits)


def body(queries, keys, values, outputs, grad_out, lse, tile_slot, tile_live, tile_bits):
    oq, ok, ov = fused(
        queries[0], grad_out[0], outputs[0], keys[0], values[0], lse[0], tile_slot, tile_live, tile_bits[0, 0]
    )
    return oq[None], ok[None], ov[None]


def solution(mesh):
    in_specs = (
        P("row", "col", None),
        P("col", "row", None),
        P("col", "row", None),
        P("row", "col", None),
        P("row", "col", None),
        P("row", None, None),
        P("row", "col", None),
        P("row", "col"),
        P("row", "col", None, None, None),
    )
    out_specs = (P("row", "col", None), P("col", "row", None), P("col", "row", None))
    return jax.shard_map(body, mesh=mesh, in_specs=in_specs, out_specs=out_specs, check_vma=False)
```

```python
import functools
import math

import jax
import jax.numpy as jnp
from jax import lax
from jax.experimental import pallas as pl
from jax.experimental.pallas import tpu as pltpu
from jax.sharding import PartitionSpec as P

MESH = pl.DeviceIdType.MESH
RING = 8
PIECE = 32
NEG = -1e30
F32 = jnp.float32
BF16 = jnp.bfloat16


def places():
    r, col = lax.axis_index("row"), lax.axis_index("col")
    xl, z = r // RING, lax.rem(r, RING)
    c = lax.rem(col, 2)
    y = lax.rem(col // 2, RING)
    xh = col // (2 * RING)
    return xl, z, xh, y, c


def turn(a, d):
    return lax.rem(a + d + RING, RING)


def piece(n):
    return pl.ds(pl.multiple_of(n * PIECE, PIECE), PIECE)


def q_rows(xh, y, c):
    return pl.ds(pl.multiple_of((xh * 16 + y * 2 + c) * PIECE, PIECE), PIECE)


def k_rows(xl, z):
    return pl.ds(pl.multiple_of((xl * 8 + z) * PIECE, PIECE), PIECE)


CHAIN = {1: 0, 2: 1, 3: 2, 4: 3, -1: 0, -2: -1, -3: -2}
DEEP = {1: 0, 2: 0, 3: 2, 4: 3, -1: 0, -2: -1, -3: -2}
FLAT = {1: 0, 2: 1, 3: 0, 4: 3, -1: 0, -2: 0, -3: -2}


def mirror(tree):
    return {-child: -parent for child, parent in tree.items()}


def neighbours(xl, z, xh, y, c):
    near = {"core": {"col": xh * 16 + y * 2 + 1 - c}}
    for far in range(-3, 4):
        for other in range(2):
            if far == 0 and other == 0:
                continue
            x = 1 - xh if other else xh
            near["q", other, far] = {"col": x * 16 + turn(y, far) * 2 + c}
            x = 1 - xl if other else xl
            near["k", other, far] = {"row": x * 8 + turn(z, far)}
    return near


def greet(near):
    barrier = pltpu.get_barrier_semaphore()
    for where in near:
        pl.semaphore_signal(barrier, inc=1, device_id=where, device_id_type=MESH)
    pl.semaphore_wait(barrier, len(near))


class Post:
    def __init__(self, send, recv):
        self.send, self.recv, self.count, self.sent = send, recv, 0, []

    def slot(self):
        self.count += 1
        return self.count - 1

    def put(self, slot, src, dst, where):
        copy = pltpu.make_async_remote_copy(
            src_ref=src,
            dst_ref=dst,
            send_sem=self.send.at[slot],
            recv_sem=self.recv.at[slot],
            device_id=where,
            device_id_type=MESH,
        )
        copy.start()
        self.sent.append(copy)

    def got(self, slot, dst):
        pltpu.make_async_copy(dst, dst, self.recv.at[slot]).wait()

    def finish(self):
        for copy in self.sent:
            copy.wait_send()


OWN_TREE, MATE_TREE = CHAIN, CHAIN


def fused_kernel(
    q, g, o, k, v, lse_in, slots_in, live_in, bits_in,
    oq, ok, ov,
    qa, ga, ka, va, o_s, lse, bits, slots, live,
    bias, delta_t, qt, gt, kc, vc, kt, prob, score,
    dqp, dkv, core_land, kv_leaf, kv_mine, kv_root, q_leaf, q_mine, q_root,
    load_sem, send, recv,
):
    xl, z, xh, y, c = places()
    near = neighbours(xl, z, xh, y, c)
    rows, keys = qa.shape[1], ka.shape[1]
    scale = 0.125

    my_q, my_k = q_rows(xh, y, c), k_rows(xl, z)
    loads = {}

    def load(name, pairs):
        made = []
        for src, dst in pairs:
            copy = pltpu.make_async_copy(src, dst, load_sem.at[load.count])
            load.count += 1
            copy.start()
            made.append(copy)
        loads[name] = made

    def loaded(*names):
        for name in names:
            for copy in loads[name]:
                copy.wait()

    load.count = 0
    for name, src, full, where in (("k", k, ka, my_k), ("q", q, qa, my_q), ("v", v, va, my_k), ("g", g, ga, my_q)):
        load(name, [(src.at[:, p * 128 : p * 128 + 128], full.at[p, where, :]) for p in range(4)])
    load("o", [(o.at[:, p * 128 : p * 128 + 128], o_s.at[p]) for p in range(4)])
    load("tables", [(slots_in, slots), (live_in, live), (bits_in, bits)])
    load("lse", [(lse_in, lse)])

    greet([near["core"]] + [near[kind, other, far] for kind in "kq" for other, far in ((1, 0), (0, 1), (0, -1))])
    post = Post(send, recv)

    streams = {}
    for name, kind, full, place, flip in (
        ("k", "k", ka, (xl, z), False),
        ("q", "q", qa, (xh, y), False),
        ("v", "k", va, (xl, z), True),
        ("g", "q", ga, (xh, y), True),
    ):
        trees = [mirror(t) if flip else t for t in (OWN_TREE, MATE_TREE)]
        st = dict(kind=kind, full=full, pos=place[0], ring=place[1], trees=trees, slots={}, core={}, mate=post.slot())
        st["rows"] = q_rows if kind == "q" else (lambda x, t, core: k_rows(x, t))
        for s in range(2):
            for d in trees[s]:
                st["slots"][s, d] = post.slot()
            if kind == "q":
                for d in (0, *trees[s]):
                    st["core"][s, d] = post.slot()
        streams[name] = st

    def piece_of(st, s, shift, core):
        pos = st["pos"] if s == 0 else 1 - st["pos"]
        return st["full"].at[:, st["rows"](pos, turn(st["ring"], -shift), core), :]

    def pass_on(st, s, d):
        ref = piece_of(st, s, d, c)
        for child, parent in sorted(st["trees"][s].items(), key=lambda e: -abs(e[0] - e[1])):
            if parent == d:
                post.put(st["slots"][s, child], ref, ref, near[st["kind"], 0, child - parent])
        if st["kind"] == "q":
            post.put(st["core"][s, d], ref, ref, near["core"])

    def begin(st):
        ref = piece_of(st, 0, 0, c)
        post.put(st["mate"], ref, ref, near[st["kind"], 1, 0])
        pass_on(st, 0, 0)

    def arrive(st, s, d):
        if (s, d) == (1, 0):
            post.got(st["mate"], piece_of(st, 1, 0, c))
        else:
            post.got(st["slots"][s, d], piece_of(st, s, d, c))
        pass_on(st, s, d)

    def arrivals():
        found = []
        for n, name in enumerate(("k", "q", "v", "g")):
            for s in range(2):
                for d in ((0,) if s else ()) + tuple(streams[name]["trees"][s]):
                    found.append((abs(d) + s, -s, n, -d, name, d))
        return [(name, -s, d) for _, s, _, _, name, d in sorted(found)]

    for name in ("k", "q", "v"):
        loaded(name)
        begin(streams[name])
    loaded("g", "o")
    lane = lax.broadcasted_iota(jnp.int32, (PIECE, 128), 1)
    delta = jnp.zeros((PIECE, 128), F32)
    for p in range(4):
        product = ga[p, my_q, :].astype(F32) * o_s[p].astype(F32)
        for a in range(2):
            one = jnp.sum(product[:, a * 64 : a * 64 + 64], axis=1, keepdims=True)
            delta = jnp.where(lane == 2 * p + a, one, delta)
    ga[4, my_q, :] = delta.astype(BF16)
    begin(streams["g"])

    loaded("tables")
    bit_of = lax.broadcasted_iota(jnp.int32, (16, 128), 0)
    listed = live[0, 0]

    @pl.loop(0, 32)
    def _(t):
        entry, valid = jnp.int32(0), jnp.int32(0)
        for e in range(24):
            hit = jnp.logical_and(slots[0, 0, e] == t, e < listed)
            entry = jnp.where(hit, jnp.int32(e), entry)
            valid = jnp.where(hit, jnp.int32(1), valid)
        words = bits[entry] * valid
        across = pl.multiple_of((t // 4) * 128, 128)
        down = pl.multiple_of(lax.rem(t, 4) * 128, 128)
        for r in range(8):
            word = jnp.broadcast_to(words[r : r + 1, :], (16, 128))
            edge = jnp.bitwise_and(jnp.right_shift(word, bit_of), 1)
            bias[pl.ds(down + r * 16, 16), pl.ds(across, 128)] = jnp.where(edge == 1, 0.0, NEG)

    for name, s, d in arrivals():
        arrive(streams[name], s, d)
    for n in ("q", "g"):
        st = streams[n]
        for (s, shift), slot in st["core"].items():
            post.got(slot, piece_of(st, s, shift, 1 - c))
    loaded("lse")

    trees = (FLAT, mirror(FLAT))
    leaves = [[d for d in t if d not in t.values() and t[d] != 0] for t in trees]
    tops = [[d for d in t if t[d] == 0] for t in trees]
    book = []
    for p in range(4):
        entry = dict(core=post.slot())
        for kind in ("kv", "q"):
            for n in range(2):
                for d in leaves[n]:
                    entry[kind, n, "leaf", d] = post.slot()
                for b in range(2) if kind == "kv" else (n,):
                    for d in tops[n] + ([0] if b == 1 else []):
                        entry[kind, n, b, d] = post.slot()
        book.append(entry)

    def child_of(n, d):
        found = [e for e, up in trees[n].items() if up == d]
        return found[0] if found else None

    def kv_top(p, n, b, d, src):
        dst = kv_root.at[p, n, b, tops[n].index(d) if d else 4]
        post.put(book[p]["kv", n, b, d], src, dst, near["k", b, -d])

    def kv_side(b):
        return xl if b == 0 else 1 - xl

    def scatter_start(p):
        post.put(book[p]["core"], dqp.at[p, :, :, 1 - c], core_land.at[p], near["core"])
        for n in range(2):
            for i, d in enumerate(leaves[n]):
                src = dkv.at[p, 2 * n : 2 * n + 2, piece(turn(z, -d)), :]
                post.put(book[p]["kv", n, "leaf", d], src, kv_leaf.at[p, n, i], near["k", 0, trees[n][d] - d])
            for d in tops[n]:
                if child_of(n, d) is None:
                    for b in range(2):
                        kv_top(p, n, b, d, dkv.at[p, 2 * n + kv_side(b), piece(turn(z, -d)), :])
            kv_top(p, n, 1, 0, dkv.at[p, 2 * n + kv_side(1), piece(z), :])

    def kv_middle(p):
        for n in range(2):
            for j, d in enumerate(tops[n]):
                e = child_of(n, d)
                if e is None:
                    continue
                i = leaves[n].index(e)
                post.got(book[p]["kv", n, "leaf", e], kv_leaf.at[p, n, i])
                own = dkv[p, 2 * n : 2 * n + 2, piece(turn(z, -d)), :].astype(F32)
                kv_mine[p, n, j] = (own + kv_leaf[p, n, i].astype(F32)).astype(BF16)
                for b in range(2):
                    kv_top(p, n, b, d, kv_mine.at[p, n, j, kv_side(b)])

    def kv_final(p):
        for n, out in enumerate((ok, ov)):
            total = dkv[p, 2 * n + xl, piece(z), :].astype(F32)
            for b in range(2):
                for d in tops[n] + ([0] if b == 1 else []):
                    i = tops[n].index(d) if d else 4
                    post.got(book[p]["kv", n, b, d], kv_root.at[p, n, b, i])
                    total = total + kv_root[p, n, b, i].astype(F32)
            out[:, p * 128 : p * 128 + 128] = total.astype(BF16)

    def q_own(p, b, t):
        side = xh if b == 0 else 1 - xh
        return dqp[p, side, t, c].astype(F32) + core_land[p, side, t].astype(F32)

    def q_put(p, b, d, total):
        i = (leaves[b] + tops[b] + [0]).index(d)
        q_mine[p, b, i] = total.astype(BF16)
        if d in leaves[b]:
            slot, dst = book[p]["q", b, "leaf", d], q_leaf.at[p, b, i]
            post.put(slot, q_mine.at[p, b, i], dst, near["q", 0, trees[b][d] - d])
        else:
            dst = q_root.at[p, b, i - len(leaves[b])]
            post.put(book[p]["q", b, b, d], q_mine.at[p, b, i], dst, near["q", b, -d])

    def q_first(p):
        post.got(book[p]["core"], core_land.at[p])
        for b in range(2):
            for d in leaves[b] + [d for d in tops[b] if child_of(b, d) is None]:
                q_put(p, b, d, q_own(p, b, turn(y, -d)))
        q_put(p, 1, 0, q_own(p, 1, y))

    def q_middle(p):
        for b in range(2):
            for d in tops[b]:
                e = child_of(b, d)
                if e is None:
                    continue
                i = leaves[b].index(e)
                post.got(book[p]["q", b, "leaf", e], q_leaf.at[p, b, i])
                q_put(p, b, d, q_own(p, b, turn(y, -d)) + q_leaf[p, b, i].astype(F32))

    def q_final(p):
        total = q_own(p, 0, y)
        for b in range(2):
            for d in tops[b] + ([0] if b == 1 else []):
                i = tops[b].index(d) if d else 4
                post.got(book[p]["q", b, b, d], q_root.at[p, b, i])
                total = total + q_root[p, b, i].astype(F32)
        oq[:, p * 128 : p * 128 + 128] = total.astype(BF16)

    delta_t[...] = ga[4].astype(F32).T
    lane = lax.broadcasted_iota(jnp.int32, (keys, 128), 1)
    row = lax.broadcasted_iota(jnp.int32, (16, rows), 0)
    for p in range(4):
        kp = ka[p].astype(F32)
        vp = va[p].astype(F32)
        qp_t = qa[p].T
        gp_t = ga[p].T
        kt[...] = ka[p].T
        for a in range(2):
            own = (lane < 64) if a == 0 else (lane >= 64)
            free = 64 * (1 - a)
            kc[a] = jnp.where(own, kp, jnp.where(lane < free + 3, 1.0, 0.0)).astype(BF16)
            vc[a] = jnp.where(own, vp, jnp.where(lane < free + 1, 1.0, 0.0)).astype(BF16)
            low = lse[2 * p + a : 2 * p + a + 1, :] * (-8.0)
            first = low.astype(BF16).astype(F32)
            second = (low - first).astype(BF16).astype(F32)
            third = low - first - second
            qt[a] = qp_t
            qt[a, free : free + 16, :] = jnp.where(
                row == 0, first, jnp.where(row == 1, second, jnp.where(row == 2, third, 0.0))
            ).astype(BF16)
            gt[a] = gp_t
            gt[a, free : free + 16, :] = jnp.where(
                row == 0, -delta_t[2 * p + a : 2 * p + a + 1, :], 0.0
            ).astype(BF16)
        parts = []
        for a in range(2):
            for ib in range(rows // 256):
                for jb in range(keys // 128):
                    js, is_ = slice(jb * 128, jb * 128 + 128), slice(ib * 256, ib * 256 + 256)
                    s = jnp.dot(kc[a, js, :], qt[a, :, is_], preferred_element_type=F32)
                    w = jnp.dot(vc[a, js, :], gt[a, :, is_], preferred_element_type=F32)
                    pr = jnp.exp2(s * (scale * math.log2(math.e)) + bias[js, is_])
                    prob[js, is_] = pr.astype(BF16)
                    score[js, is_] = (pr * w).astype(BF16)
            value_sum = jnp.dot(prob[...], ga[p], preferred_element_type=F32)
            key_sum = jnp.dot(score[...], qa[p], preferred_element_type=F32)
            query_sum = jnp.dot(kt[64 * a : 64 * a + 64, :], score[...], preferred_element_type=F32)
            parts.append((value_sum, key_sum, query_sum))
            if a == 0:
                if p >= 1:
                    q_first(p - 1)
                if p >= 2:
                    kv_middle(p - 2)
        dkv[p, 0:2] = (jnp.where(lane < 64, parts[0][1], parts[1][1]) * scale).astype(BF16).reshape(2, 256, 128)
        dkv[p, 2:4] = jnp.where(lane < 64, parts[0][0], parts[1][0]).astype(BF16).reshape(2, 256, 128)
        both = jnp.concatenate([parts[0][2], parts[1][2]], axis=0) * scale
        dqp[p] = both.T.astype(BF16).reshape(2, 8, 2, PIECE, 128)
        scatter_start(p)
        if p >= 2:
            q_middle(p - 2)
        if p >= 3:
            kv_final(p - 3)
    q_first(3)
    kv_middle(2)
    q_middle(2)
    kv_middle(3)
    q_middle(3)
    for p in range(4):
        if p > 0:
            kv_final(p)
        q_final(p)
    post.finish()


COPIES = 2 * 15 + 2 * (15 + 16) + 4 * 40


def fused(q, g, o, k, v, lse, slots, live, bits):
    vmem = pl.BlockSpec(memory_space=pltpu.VMEM)
    hbm = pl.BlockSpec(memory_space=pl.ANY)
    rows, keys = 1024, 512
    return pl.pallas_call(
        fused_kernel,
        out_shape=[jax.ShapeDtypeStruct((PIECE, 512), BF16)] * 3,
        in_specs=[hbm] * 9,
        out_specs=[vmem] * 3,
        scratch_shapes=[
            pltpu.VMEM((4, rows, 128), BF16),
            pltpu.VMEM((5, rows, 128), BF16),
            pltpu.VMEM((4, keys, 128), BF16),
            pltpu.VMEM((4, keys, 128), BF16),
            pltpu.VMEM((4, PIECE, 128), BF16),
            pltpu.VMEM(lse.shape, F32),
            pltpu.VMEM(bits.shape, jnp.int32),
            pltpu.SMEM(slots.shape, jnp.int32),
            pltpu.SMEM(live.shape, jnp.int32),
            pltpu.VMEM((keys, rows), F32),
            pltpu.VMEM((128, rows), F32),
            pltpu.VMEM((2, 128, rows), BF16),
            pltpu.VMEM((2, 128, rows), BF16),
            pltpu.VMEM((2, keys, 128), BF16),
            pltpu.VMEM((2, keys, 128), BF16),
            pltpu.VMEM((128, keys), BF16),
            pltpu.VMEM((keys, rows), BF16),
            pltpu.VMEM((keys, rows), BF16),
            pltpu.VMEM((4, 2, 8, 2, PIECE, 128), BF16),
            pltpu.VMEM((4, 4, 256, 128), BF16),
            pltpu.VMEM((4, 2, 8, PIECE, 128), BF16),
            pltpu.VMEM((4, 2, 3, 2, PIECE, 128), BF16),
            pltpu.VMEM((4, 2, 4, 2, PIECE, 128), BF16),
            pltpu.VMEM((4, 2, 2, 5, PIECE, 128), BF16),
            pltpu.VMEM((4, 2, 3, PIECE, 128), BF16),
            pltpu.VMEM((4, 2, 8, PIECE, 128), BF16),
            pltpu.VMEM((4, 2, 5, PIECE, 128), BF16),
            pltpu.SemaphoreType.DMA((24,)),
            pltpu.SemaphoreType.DMA((COPIES,)),
            pltpu.SemaphoreType.DMA((COPIES,)),
        ],
        compiler_params=pltpu.CompilerParams(
            collective_id=0, has_side_effects=True, vmem_limit_bytes=56 << 20
        ),
        name="fused",
    )(q, g, o, k, v, lse, slots, live, bits)


def body(queries, keys, values, outputs, grad_out, lse, tile_slot, tile_live, tile_bits):
    oq, ok, ov = fused(
        queries[0], grad_out[0], outputs[0], keys[0], values[0], lse[0], tile_slot, tile_live, tile_bits[0, 0]
    )
    return oq[None], ok[None], ov[None]


def solution(mesh):
    in_specs = (
        P("row", "col", None),
        P("col", "row", None),
        P("col", "row", None),
        P("row", "col", None),
        P("row", "col", None),
        P("row", None, None),
        P("row", "col", None),
        P("row", "col"),
        P("row", "col", None, None, None),
    )
    out_specs = (P("row", "col", None), P("col", "row", None), P("col", "row", None))
    return jax.shard_map(body, mesh=mesh, in_specs=in_specs, out_specs=out_specs, check_vma=False)
```

```python
import functools
import math

import jax
import jax.numpy as jnp
from jax import lax
from jax.experimental import pallas as pl
from jax.experimental.pallas import tpu as pltpu
from jax.sharding import PartitionSpec as P

MESH = pl.DeviceIdType.MESH
RING = 8
PIECE = 32
NEG = -1e30
F32 = jnp.float32
BF16 = jnp.bfloat16


def places():
    r, col = lax.axis_index("row"), lax.axis_index("col")
    xl, z = r // RING, lax.rem(r, RING)
    c = lax.rem(col, 2)
    y = lax.rem(col // 2, RING)
    xh = col // (2 * RING)
    return xl, z, xh, y, c


def turn(a, d):
    return lax.rem(a + d + RING, RING)


def piece(n):
    return pl.ds(pl.multiple_of(n * PIECE, PIECE), PIECE)


def q_rows(xh, y, c):
    return pl.ds(pl.multiple_of((xh * 16 + y * 2 + c) * PIECE, PIECE), PIECE)


def k_rows(xl, z):
    return pl.ds(pl.multiple_of((xl * 8 + z) * PIECE, PIECE), PIECE)


CHAIN = {1: 0, 2: 1, 3: 2, 4: 3, -1: 0, -2: -1, -3: -2}
DEEP = {1: 0, 2: 0, 3: 2, 4: 3, -1: 0, -2: -1, -3: -2}
FLAT = {1: 0, 2: 1, 3: 0, 4: 3, -1: 0, -2: 0, -3: -2}


def mirror(tree):
    return {-child: -parent for child, parent in tree.items()}


def neighbours(xl, z, xh, y, c):
    near = {"core": {"col": xh * 16 + y * 2 + 1 - c}}
    for far in range(-3, 4):
        for other in range(2):
            if far == 0 and other == 0:
                continue
            x = 1 - xh if other else xh
            near["q", other, far] = {"col": x * 16 + turn(y, far) * 2 + c}
            x = 1 - xl if other else xl
            near["k", other, far] = {"row": x * 8 + turn(z, far)}
    return near


def greet(near):
    barrier = pltpu.get_barrier_semaphore()
    for where in near:
        pl.semaphore_signal(barrier, inc=1, device_id=where, device_id_type=MESH)
    pl.semaphore_wait(barrier, len(near))


class Post:
    def __init__(self, send, recv):
        self.send, self.recv, self.count, self.sent = send, recv, 0, []

    def slot(self):
        self.count += 1
        return self.count - 1

    def put(self, slot, src, dst, where):
        copy = pltpu.make_async_remote_copy(
            src_ref=src,
            dst_ref=dst,
            send_sem=self.send.at[slot],
            recv_sem=self.recv.at[slot],
            device_id=where,
            device_id_type=MESH,
        )
        copy.start()
        self.sent.append(copy)

    def got(self, slot, dst):
        pltpu.make_async_copy(dst, dst, self.recv.at[slot]).wait()

    def finish(self):
        for copy in self.sent:
            copy.wait_send()


OWN_TREE, MATE_TREE = CHAIN, CHAIN


def fused_kernel(
    q, g, o, k, v, lse_in, slots_in, live_in, bits_in,
    result,
    qa, ga, ka, va, o_s, lse, bits, slots, live,
    bias, delta_t, qt, gt, kc, vc, kt, prob, score,
    dqp, dkv, core_land, kv_leaf, kv_mine, kv_root, q_leaf, q_mine, q_root,
    load_sem, send, recv,
):
    xl, z, xh, y, c = places()
    near = neighbours(xl, z, xh, y, c)
    oq, ok, ov = result.at[0], result.at[1], result.at[2]
    rows, keys = qa.shape[1], ka.shape[1]
    scale = 0.125

    my_q, my_k = q_rows(xh, y, c), k_rows(xl, z)
    loads = {}

    def load(name, pairs):
        made = []
        for src, dst in pairs:
            copy = pltpu.make_async_copy(src, dst, load_sem.at[load.count])
            load.count += 1
            copy.start()
            made.append(copy)
        loads[name] = made

    def loaded(*names):
        for name in names:
            for copy in loads[name]:
                copy.wait()

    load.count = 0
    for name, src, full, where in (("k", k, ka, my_k), ("q", q, qa, my_q), ("v", v, va, my_k), ("g", g, ga, my_q)):
        load(name, [(src.at[:, p * 128 : p * 128 + 128], full.at[p, where, :]) for p in range(4)])
    load("o", [(o.at[:, p * 128 : p * 128 + 128], o_s.at[p]) for p in range(4)])
    load("tables", [(slots_in, slots), (live_in, live), (bits_in, bits)])
    load("lse", [(lse_in, lse)])

    greet([near["core"]] + [near[kind, other, far] for kind in "kq" for other, far in ((1, 0), (0, 1), (0, -1))])
    post = Post(send, recv)

    streams = {}
    for name, kind, full, place, flip in (
        ("k", "k", ka, (xl, z), False),
        ("q", "q", qa, (xh, y), False),
        ("v", "k", va, (xl, z), True),
        ("g", "q", ga, (xh, y), True),
    ):
        trees = [mirror(t) if flip else t for t in (OWN_TREE, MATE_TREE)]
        st = dict(kind=kind, full=full, pos=place[0], ring=place[1], trees=trees, slots={}, core={}, mate=post.slot())
        st["rows"] = q_rows if kind == "q" else (lambda x, t, core: k_rows(x, t))
        for s in range(2):
            for d in trees[s]:
                st["slots"][s, d] = post.slot()
            if kind == "q":
                for d in (0, *trees[s]):
                    st["core"][s, d] = post.slot()
        streams[name] = st

    def piece_of(st, s, shift, core):
        pos = st["pos"] if s == 0 else 1 - st["pos"]
        return st["full"].at[:, st["rows"](pos, turn(st["ring"], -shift), core), :]

    def pass_on(st, s, d):
        ref = piece_of(st, s, d, c)
        for child, parent in sorted(st["trees"][s].items(), key=lambda e: -abs(e[0] - e[1])):
            if parent == d:
                post.put(st["slots"][s, child], ref, ref, near[st["kind"], 0, child - parent])
        if st["kind"] == "q":
            post.put(st["core"][s, d], ref, ref, near["core"])

    def begin(st):
        ref = piece_of(st, 0, 0, c)
        post.put(st["mate"], ref, ref, near[st["kind"], 1, 0])
        pass_on(st, 0, 0)

    def arrive(st, s, d):
        if (s, d) == (1, 0):
            post.got(st["mate"], piece_of(st, 1, 0, c))
        else:
            post.got(st["slots"][s, d], piece_of(st, s, d, c))
        pass_on(st, s, d)

    def arrivals():
        found = []
        for n, name in enumerate(("k", "q", "v", "g")):
            for s in range(2):
                for d in ((0,) if s else ()) + tuple(streams[name]["trees"][s]):
                    found.append((abs(d) + s, -s, n, -d, name, d))
        return [(name, -s, d) for _, s, _, _, name, d in sorted(found)]

    for name in ("k", "q", "v"):
        loaded(name)
        begin(streams[name])
    loaded("g", "o")
    lane = lax.broadcasted_iota(jnp.int32, (PIECE, 128), 1)
    delta = jnp.zeros((PIECE, 128), F32)
    for p in range(4):
        product = ga[p, my_q, :].astype(F32) * o_s[p].astype(F32)
        for a in range(2):
            one = jnp.sum(product[:, a * 64 : a * 64 + 64], axis=1, keepdims=True)
            delta = jnp.where(lane == 2 * p + a, one, delta)
    ga[4, my_q, :] = delta.astype(BF16)
    begin(streams["g"])

    loaded("tables")
    bit_of = lax.broadcasted_iota(jnp.int32, (16, 128), 0)
    listed = live[0, 0]

    @pl.loop(0, 32)
    def _(t):
        entry, valid = jnp.int32(0), jnp.int32(0)
        for e in range(24):
            hit = jnp.logical_and(slots[0, 0, e] == t, e < listed)
            entry = jnp.where(hit, jnp.int32(e), entry)
            valid = jnp.where(hit, jnp.int32(1), valid)
        words = bits[entry] * valid
        across = pl.multiple_of((t // 4) * 128, 128)
        down = pl.multiple_of(lax.rem(t, 4) * 128, 128)
        for r in range(8):
            word = jnp.broadcast_to(words[r : r + 1, :], (16, 128))
            edge = jnp.bitwise_and(jnp.right_shift(word, bit_of), 1)
            bias[pl.ds(down + r * 16, 16), pl.ds(across, 128)] = jnp.where(edge == 1, 0.0, NEG)

    for name, s, d in arrivals():
        arrive(streams[name], s, d)
    for n in ("q", "g"):
        st = streams[n]
        for (s, shift), slot in st["core"].items():
            post.got(slot, piece_of(st, s, shift, 1 - c))
    loaded("lse")

    trees = (FLAT, mirror(FLAT))
    leaves = [[d for d in t if d not in t.values() and t[d] != 0] for t in trees]
    tops = [[d for d in t if t[d] == 0] for t in trees]
    book = []
    for p in range(4):
        entry = dict(core=post.slot())
        for kind in ("kv", "q"):
            for n in range(2):
                for d in leaves[n]:
                    entry[kind, n, "leaf", d] = post.slot()
                for b in range(2) if kind == "kv" else (n,):
                    for d in tops[n] + ([0] if b == 1 else []):
                        entry[kind, n, b, d] = post.slot()
        book.append(entry)

    def child_of(n, d):
        found = [e for e, up in trees[n].items() if up == d]
        return found[0] if found else None

    def kv_top(p, n, b, d, src):
        dst = kv_root.at[p, n, b, tops[n].index(d) if d else 4]
        post.put(book[p]["kv", n, b, d], src, dst, near["k", b, -d])

    def kv_side(b):
        return xl if b == 0 else 1 - xl

    def scatter_start(p):
        post.put(book[p]["core"], dqp.at[p, :, :, 1 - c], core_land.at[p], near["core"])
        for n in range(2):
            for i, d in enumerate(leaves[n]):
                src = dkv.at[p, 2 * n : 2 * n + 2, piece(turn(z, -d)), :]
                post.put(book[p]["kv", n, "leaf", d], src, kv_leaf.at[p, n, i], near["k", 0, trees[n][d] - d])
            for d in tops[n]:
                if child_of(n, d) is None:
                    for b in range(2):
                        kv_top(p, n, b, d, dkv.at[p, 2 * n + kv_side(b), piece(turn(z, -d)), :])
            kv_top(p, n, 1, 0, dkv.at[p, 2 * n + kv_side(1), piece(z), :])

    def kv_middle(p):
        for n in range(2):
            for j, d in enumerate(tops[n]):
                e = child_of(n, d)
                if e is None:
                    continue
                i = leaves[n].index(e)
                post.got(book[p]["kv", n, "leaf", e], kv_leaf.at[p, n, i])
                own = dkv[p, 2 * n : 2 * n + 2, piece(turn(z, -d)), :].astype(F32)
                kv_mine[p, n, j] = (own + kv_leaf[p, n, i].astype(F32)).astype(BF16)
                for b in range(2):
                    kv_top(p, n, b, d, kv_mine.at[p, n, j, kv_side(b)])

    def kv_final(p):
        for n, out in enumerate((ok, ov)):
            total = dkv[p, 2 * n + xl, piece(z), :].astype(F32)
            for b in range(2):
                for d in tops[n] + ([0] if b == 1 else []):
                    i = tops[n].index(d) if d else 4
                    post.got(book[p]["kv", n, b, d], kv_root.at[p, n, b, i])
                    total = total + kv_root[p, n, b, i].astype(F32)
            out[:, p * 128 : p * 128 + 128] = total.astype(BF16)

    def q_own(p, b, t):
        side = xh if b == 0 else 1 - xh
        return dqp[p, side, t, c].astype(F32) + core_land[p, side, t].astype(F32)

    def q_put(p, b, d, total):
        i = (leaves[b] + tops[b] + [0]).index(d)
        q_mine[p, b, i] = total.astype(BF16)
        if d in leaves[b]:
            slot, dst = book[p]["q", b, "leaf", d], q_leaf.at[p, b, i]
            post.put(slot, q_mine.at[p, b, i], dst, near["q", 0, trees[b][d] - d])
        else:
            dst = q_root.at[p, b, i - len(leaves[b])]
            post.put(book[p]["q", b, b, d], q_mine.at[p, b, i], dst, near["q", b, -d])

    def q_first(p):
        post.got(book[p]["core"], core_land.at[p])
        for b in range(2):
            for d in leaves[b] + [d for d in tops[b] if child_of(b, d) is None]:
                q_put(p, b, d, q_own(p, b, turn(y, -d)))
        q_put(p, 1, 0, q_own(p, 1, y))

    def q_middle(p):
        for b in range(2):
            for d in tops[b]:
                e = child_of(b, d)
                if e is None:
                    continue
                i = leaves[b].index(e)
                post.got(book[p]["q", b, "leaf", e], q_leaf.at[p, b, i])
                q_put(p, b, d, q_own(p, b, turn(y, -d)) + q_leaf[p, b, i].astype(F32))

    def q_final(p):
        total = q_own(p, 0, y)
        for b in range(2):
            for d in tops[b] + ([0] if b == 1 else []):
                i = tops[b].index(d) if d else 4
                post.got(book[p]["q", b, b, d], q_root.at[p, b, i])
                total = total + q_root[p, b, i].astype(F32)
        oq[:, p * 128 : p * 128 + 128] = total.astype(BF16)

    delta_t[...] = ga[4].astype(F32).T
    lane = lax.broadcasted_iota(jnp.int32, (keys, 128), 1)
    row = lax.broadcasted_iota(jnp.int32, (16, rows), 0)
    for p in range(4):
        kp = ka[p].astype(F32)
        vp = va[p].astype(F32)
        qp_t = qa[p].T
        gp_t = ga[p].T
        kt[...] = ka[p].T
        for a in range(2):
            own = (lane < 64) if a == 0 else (lane >= 64)
            free = 64 * (1 - a)
            kc[a] = jnp.where(own, kp, jnp.where(lane < free + 3, 1.0, 0.0)).astype(BF16)
            vc[a] = jnp.where(own, vp, jnp.where(lane < free + 1, 1.0, 0.0)).astype(BF16)
            low = lse[2 * p + a : 2 * p + a + 1, :] * (-8.0)
            first = low.astype(BF16).astype(F32)
            second = (low - first).astype(BF16).astype(F32)
            third = low - first - second
            qt[a] = qp_t
            qt[a, free : free + 16, :] = jnp.where(
                row == 0, first, jnp.where(row == 1, second, jnp.where(row == 2, third, 0.0))
            ).astype(BF16)
            gt[a] = gp_t
            gt[a, free : free + 16, :] = jnp.where(
                row == 0, -delta_t[2 * p + a : 2 * p + a + 1, :], 0.0
            ).astype(BF16)
        parts = []
        for a in range(2):
            for ib in range(rows // 256):
                for jb in range(keys // 128):
                    js, is_ = slice(jb * 128, jb * 128 + 128), slice(ib * 256, ib * 256 + 256)
                    s = jnp.dot(kc[a, js, :], qt[a, :, is_], preferred_element_type=F32)
                    w = jnp.dot(vc[a, js, :], gt[a, :, is_], preferred_element_type=F32)
                    pr = jnp.exp2(s * (scale * math.log2(math.e)) + bias[js, is_])
                    prob[js, is_] = pr.astype(BF16)
                    score[js, is_] = (pr * w).astype(BF16)
            value_sum = jnp.dot(prob[...], ga[p], preferred_element_type=F32)
            key_sum = jnp.dot(score[...], qa[p], preferred_element_type=F32)
            query_sum = jnp.dot(kt[64 * a : 64 * a + 64, :], score[...], preferred_element_type=F32)
            parts.append((value_sum, key_sum, query_sum))
            if a == 0:
                if p >= 1:
                    q_first(p - 1)
                if p >= 2:
                    kv_middle(p - 2)
        dkv[p, 0:2] = (jnp.where(lane < 64, parts[0][1], parts[1][1]) * scale).astype(BF16).reshape(2, 256, 128)
        dkv[p, 2:4] = jnp.where(lane < 64, parts[0][0], parts[1][0]).astype(BF16).reshape(2, 256, 128)
        both = jnp.concatenate([parts[0][2], parts[1][2]], axis=0) * scale
        dqp[p] = both.T.astype(BF16).reshape(2, 8, 2, PIECE, 128)
        scatter_start(p)
        if p >= 2:
            q_middle(p - 2)
        if p >= 3:
            kv_final(p - 3)
    q_first(3)
    kv_middle(2)
    q_middle(2)
    kv_middle(3)
    q_middle(3)
    for p in range(4):
        if p > 0:
            kv_final(p)
        q_final(p)
    post.finish()


COPIES = 2 * 15 + 2 * (15 + 16) + 4 * 40


def fused(q, g, o, k, v, lse, slots, live, bits):
    vmem = pl.BlockSpec(memory_space=pltpu.VMEM)
    hbm = pl.BlockSpec(memory_space=pl.ANY)
    rows, keys = 1024, 512
    return pl.pallas_call(
        fused_kernel,
        out_shape=jax.ShapeDtypeStruct((3, PIECE, 512), BF16),
        in_specs=[hbm] * 9,
        out_specs=vmem,
        scratch_shapes=[
            pltpu.VMEM((4, rows, 128), BF16),
            pltpu.VMEM((5, rows, 128), BF16),
            pltpu.VMEM((4, keys, 128), BF16),
            pltpu.VMEM((4, keys, 128), BF16),
            pltpu.VMEM((4, PIECE, 128), BF16),
            pltpu.VMEM(lse.shape, F32),
            pltpu.VMEM(bits.shape, jnp.int32),
            pltpu.SMEM(slots.shape, jnp.int32),
            pltpu.SMEM(live.shape, jnp.int32),
            pltpu.VMEM((keys, rows), F32),
            pltpu.VMEM((128, rows), F32),
            pltpu.VMEM((2, 128, rows), BF16),
            pltpu.VMEM((2, 128, rows), BF16),
            pltpu.VMEM((2, keys, 128), BF16),
            pltpu.VMEM((2, keys, 128), BF16),
            pltpu.VMEM((128, keys), BF16),
            pltpu.VMEM((keys, rows), BF16),
            pltpu.VMEM((keys, rows), BF16),
            pltpu.VMEM((4, 2, 8, 2, PIECE, 128), BF16),
            pltpu.VMEM((4, 4, 256, 128), BF16),
            pltpu.VMEM((4, 2, 8, PIECE, 128), BF16),
            pltpu.VMEM((4, 2, 3, 2, PIECE, 128), BF16),
            pltpu.VMEM((4, 2, 4, 2, PIECE, 128), BF16),
            pltpu.VMEM((4, 2, 2, 5, PIECE, 128), BF16),
            pltpu.VMEM((4, 2, 3, PIECE, 128), BF16),
            pltpu.VMEM((4, 2, 8, PIECE, 128), BF16),
            pltpu.VMEM((4, 2, 5, PIECE, 128), BF16),
            pltpu.SemaphoreType.DMA((24,)),
            pltpu.SemaphoreType.DMA((COPIES,)),
            pltpu.SemaphoreType.DMA((COPIES,)),
        ],
        compiler_params=pltpu.CompilerParams(
            collective_id=0, has_side_effects=True, vmem_limit_bytes=56 << 20
        ),
        name="fused",
    )(q, g, o, k, v, lse, slots, live, bits)


def body(queries, keys, values, outputs, grad_out, lse, tile_slot, tile_live, tile_bits):
    result = fused(
        queries[0], grad_out[0], outputs[0], keys[0], values[0], lse[0], tile_slot, tile_live, tile_bits[0, 0]
    )
    return result[0:1], result[1:2], result[2:3]


def solution(mesh):
    in_specs = (
        P("row", "col", None),
        P("col", "row", None),
        P("col", "row", None),
        P("row", "col", None),
        P("row", "col", None),
        P("row", None, None),
        P("row", "col", None),
        P("row", "col"),
        P("row", "col", None, None, None),
    )
    out_specs = (P("row", "col", None), P("col", "row", None), P("col", "row", None))
    return jax.shard_map(body, mesh=mesh, in_specs=in_specs, out_specs=out_specs, check_vma=False)
```
